128 devices in a mesh: kv: 2 (over core), seq: 64 (over z, y, x), dp: 1.
Axes of the slice: x: 4, y: 4, z: 4, core: 2. Of those that a mesh axis runs over, the one named last changes fastest.
Arguments:
- token_input_state: bfloat16 [4, 8192], P('dp'), may hold values from -6 to 6
- query_matrix: bfloat16 [8192, 2048], P('seq', 'kv'), may hold values from -0.0625 to 0.0625
- key_value_weight: bfloat16 [8192, 512], P('seq', 'kv'), may hold values from -0.5 to 0.5
- output_weight: bfloat16 [2048, 8192], P('kv', 'seq'), may hold values from -0.125 to 0.125
- key_cache_rows: bfloat16 [4, 2, 131072, 128], P('dp', 'kv', 'seq'), may hold values from -6000 to 6000, as said below
- value_cache_rows: bfloat16 [4, 2, 131072, 128], P('dp', 'kv', 'seq'), may hold values from -24 to 24
- live_lengths: int32 [4, 64], P('dp'), may hold values from 2 to 2048, as said below
- owner_shard: int32 [4], P('dp'), may hold values from 0 to 63
Outputs:
- layer_out: bfloat16 [4, 8192], P('dp', 'seq')
The draws below stay inside these ranges and needn't reach their ends.
Inputs may be any that keep to these rules, and one draw needn't show every extreme that they name: `live_lengths`: every block holds 2 to 2048 live slots; the owner's block of a sequence holds fewer than 2048; in every sequence some other block holds exactly 2048. `key_cache_rows`: bounded as stated.
All inputs are finite; a program needn't handle non-finite values.
Results may differ from the reference program's by a relative error of at most 0.015.
The reference program's roundings to bfloat16 on the way (of `attended`) count: a program that leaves them out, or rounds other values in their place, can miss the bound.
Values may be sent and summed in bfloat16 or wider, within the bound.
No kernel may reach another device: no remote copies, remote signals or barrier semaphores. Data moves between devices by JAX's collectives and lax.ppermute only.
A program may use at most 64 MiB of HBM per device.

```python
import math
import jax
import jax.numpy as jnp
from jax import lax

MODEL_WIDTH = 8192
HEAD_SIZE = 128
QUERY_GROUP = 8
BATCH_SEQUENCES = 4
LENGTH_PER_PART = 2048
KEY_VALUE_HEADS = 2
HQ = 16
CACHE_LENGTH = 131072
N_SEQ = 64


def lengths_and_owner(key):
    inner = jax.random.fold_in(key, 4242)
    first_key, second_key, third_key, fourth_key, fifth_key = jax.random.split(inner, 5)
    owner_shard = jax.random.randint(first_key, (BATCH_SEQUENCES,), 0, N_SEQ)
    owner_shard = jnp.where(jnp.arange(BATCH_SEQUENCES) == 0, N_SEQ - 1, owner_shard)
    first_draw = jax.random.randint(second_key, (BATCH_SEQUENCES, N_SEQ), 0, LENGTH_PER_PART)
    second_draw = jax.random.randint(third_key, (BATCH_SEQUENCES, N_SEQ), 0, LENGTH_PER_PART)
    third_draw = jax.random.randint(fourth_key, (BATCH_SEQUENCES, N_SEQ), 0, LENGTH_PER_PART)
    skewed = first_draw * second_draw // LENGTH_PER_PART * third_draw // LENGTH_PER_PART
    lengths = 2 + skewed
    lengths = jnp.minimum(lengths, LENGTH_PER_PART - 1)
    column = jnp.arange(N_SEQ)[None, :]
    extra = jax.random.randint(fifth_key, (BATCH_SEQUENCES,), 0, N_SEQ - 1)
    full_shard = (owner_shard + 1 + extra) % N_SEQ
    lengths = jnp.where(column == full_shard[:, None], LENGTH_PER_PART, lengths)
    return (lengths.astype(jnp.int32), owner_shard.astype(jnp.int32))


def draw_live_lengths(key, part):
    lengths, owner_shard = lengths_and_owner(key)
    return lengths


def draw_owner_shard(key, part):
    lengths, owner_shard = lengths_and_owner(key)
    return owner_shard


def draw_key_cache_rows(key, part):
    inner = jax.random.fold_in(key, 77)
    noise_key = jax.random.fold_in(inner, 0)
    complete_shape = (BATCH_SEQUENCES, KEY_VALUE_HEADS, N_SEQ, LENGTH_PER_PART, HEAD_SIZE)
    random_basis = jnp.clip(2.5 * jax.random.normal(noise_key, complete_shape, jnp.float32), -15.0, 15.0)
    return random_basis.reshape(BATCH_SEQUENCES, KEY_VALUE_HEADS, CACHE_LENGTH, HEAD_SIZE).astype(jnp.bfloat16)


def block_levels(rng, dims, shards, low, top_value):
    def one(dim, parts):
        steps = jax.random.uniform(jax.random.fold_in(jax.random.fold_in(rng, 6), dim), (parts,), jnp.float32, low / len(shards), top_value / len(shards))
        return jnp.repeat(jnp.exp(steps), dims[dim] // parts).reshape((-1,) + (1,) * (len(dims) - dim - 1))

    loudness = one(*shards[0])
    for cut in shards[1:]:
        loudness = loudness * one(*cut)
    return loudness


def normal_values(rng, shape, deviation, limit, cuts=(), held_as=jnp.bfloat16):
    factor_of = block_levels(rng, shape, cuts, -0.22, 0.18) if cuts else 1.0
    drawn = jax.random.normal(rng, shape, jnp.float32) * deviation * factor_of
    return jnp.minimum(jnp.maximum(drawn, -limit), limit).astype(held_as)


def setup_inputs(seed: int = 0, part: int = 0) -> dict:
    keys = jax.random.split(jax.random.key(seed), 9)
    part_splits = jax.random.split(jax.random.fold_in(keys[8], part), 9)
    token_input_state = normal_values(part_splits[0], (BATCH_SEQUENCES, MODEL_WIDTH), 1.0, 6.0)
    query_matrix = normal_values(keys[1], (MODEL_WIDTH, HQ * HEAD_SIZE), MODEL_WIDTH ** -0.5, 0.0625, ((0, 64), (1, 2)))
    key_value_weight = normal_values(keys[2], (MODEL_WIDTH, KEY_VALUE_HEADS * 2 * HEAD_SIZE), (MODEL_WIDTH // 64) ** -0.5, 0.5, ((0, 64), (1, 2)))
    output_weight = normal_values(keys[3], (HQ * HEAD_SIZE, MODEL_WIDTH), (HQ * HEAD_SIZE) ** -0.5, 0.125, ((0, 2), (1, 64)))
    key_cache_rows = draw_key_cache_rows(jax.random.fold_in(jax.random.fold_in(keys[8], part), 71), part)
    value_cache_rows = normal_values(part_splits[5], (BATCH_SEQUENCES, KEY_VALUE_HEADS, CACHE_LENGTH, HEAD_SIZE), 4.0, 24.0, ((1, 2), (2, 64)))
    live_lengths = draw_live_lengths(jax.random.fold_in(jax.random.fold_in(keys[8], part), 71), part)
    owner_shard = draw_owner_shard(jax.random.fold_in(jax.random.fold_in(keys[8], part), 71), part)
    return {"token_input_state": token_input_state, "query_matrix": query_matrix, "key_value_weight": key_value_weight, "output_weight": output_weight, "key_cache_rows": key_cache_rows, "value_cache_rows": value_cache_rows, "live_lengths": live_lengths, "owner_shard": owner_shard}


rope_theta = 500000.0

def frequencies():
    exponent = jnp.arange(0, HEAD_SIZE, 2).astype(jnp.float32) / HEAD_SIZE
    return jnp.power(rope_theta, -exponent)

def rotate(vectors, angles):
    half_size = vectors.shape[-1] // 2
    first_half = vectors[..., :half_size]
    second_half = vectors[..., half_size:]
    cosine_table = jnp.cos(angles)
    sine_table = jnp.sin(angles)
    return jnp.concatenate([first_half * cosine_table - second_half * sine_table, second_half * cosine_table + first_half * sine_table], -1)

def reference(token_input_state, query_matrix, key_value_weight, output_weight, key_cache_rows, value_cache_rows, live_lengths, owner_shard):
    query_rows = jnp.dot(token_input_state, query_matrix, preferred_element_type=jnp.float32).reshape(BATCH_SEQUENCES, KEY_VALUE_HEADS, QUERY_GROUP, HEAD_SIZE)
    key_value_rows = jnp.dot(token_input_state, key_value_weight, preferred_element_type=jnp.float32).reshape(BATCH_SEQUENCES, KEY_VALUE_HEADS, 2, HEAD_SIZE)
    lookup = jnp.take_along_axis(live_lengths, owner_shard[:, None].astype(jnp.int32), 1)[:, 0]
    position = owner_shard * LENGTH_PER_PART + lookup
    angles = position.astype(jnp.float32)[:, None] * frequencies()[None, :]
    query_rot = rotate(query_rows, angles[:, None, None, :]).astype(jnp.bfloat16)
    key_new = rotate(key_value_rows[:, :, 0], angles[:, None, :]).astype(jnp.bfloat16)
    value_new = key_value_rows[:, :, 1].astype(jnp.bfloat16)
    scaling = 1.0 / math.sqrt(HEAD_SIZE)
    key_rows = key_cache_rows.reshape(BATCH_SEQUENCES, KEY_VALUE_HEADS, N_SEQ, LENGTH_PER_PART, HEAD_SIZE)
    value_rows = value_cache_rows.reshape(BATCH_SEQUENCES, KEY_VALUE_HEADS, N_SEQ, LENGTH_PER_PART, HEAD_SIZE)
    scores = jnp.einsum('bhgd,bhsld->bhgsl', query_rot.astype(jnp.float32), key_rows.astype(jnp.float32)) * scaling
    slot_ids = jnp.arange(LENGTH_PER_PART)
    live_mask = slot_ids[None, None, :] < live_lengths[:, :, None]
    scores = jnp.where(live_mask[:, None, None], scores, -jnp.inf)
    new_score = lax.optimization_barrier(jnp.sum(query_rot.astype(jnp.float32) * key_new.astype(jnp.float32)[:, :, None, :], -1)) * scaling
    owner_mask = (owner_shard[:, None] == jnp.arange(N_SEQ)[None, :])[:, None, None, :]
    new_term = jnp.where(owner_mask, new_score[..., None], -jnp.inf)
    shard_top = jnp.maximum(lax.optimization_barrier(jnp.max(scores, -1)), new_term)
    probs = jnp.exp(scores - shard_top[..., None]).astype(jnp.bfloat16)
    new_prob = jnp.where(owner_mask, jnp.exp(new_score[..., None] - shard_top), 0.0).astype(jnp.bfloat16)
    totals = lax.optimization_barrier(jnp.sum(probs.astype(jnp.float32), -1)) + new_prob.astype(jnp.float32)
    accum = jnp.einsum('bhgsl,bhsld->bhgsd', probs.astype(jnp.float32), value_rows.astype(jnp.float32))
    accum = accum + new_prob.astype(jnp.float32)[..., None] * value_new.astype(jnp.float32)[:, :, None, None, :]
    overall = lax.optimization_barrier(jnp.max(shard_top, -1))
    factor = jnp.exp(shard_top - overall[..., None])
    attended = lax.optimization_barrier(jnp.sum(accum * factor[..., None], 3)) / lax.optimization_barrier(jnp.sum(totals * factor, 3))[..., None]
    attended = attended.astype(jnp.bfloat16).reshape(BATCH_SEQUENCES, HQ * HEAD_SIZE)
    return jnp.dot(attended, output_weight, preferred_element_type=jnp.float32).astype(jnp.bfloat16)
```

```python
import math

import jax
import jax.numpy as jnp
from jax import lax
from jax.sharding import Mesh
from jax.sharding import PartitionSpec as P

HEAD_SIZE = 128
QUERY_GROUP = 8
SEQ = ("seq_0", "seq_1", "seq_2")


rope_theta = 500000.0


def exchanges(array, axis):
    beside = lax.ppermute(array, axis, ((0, 1), (1, 0), (2, 3), (3, 2)))
    around = lax.ppermute(array, axis, ((0, 3), (3, 0), (1, 2), (2, 1)))
    across = lax.ppermute(array, axis, ((0, 2), (2, 0), (1, 3), (3, 1)))
    return (array + beside) + (around + across)


def copies_from(array, axes):
    count = lax.axis_size(axes)
    return lax.all_to_all(jnp.broadcast_to(array[None], (count, *array.shape)), axes, 0, 0, tiled=True)


def split(value, count):
    pieces = []
    for _ in range(count):
        piece = lax.reduce_precision(value, 8, 7)
        pieces.append(piece.astype(jnp.bfloat16))
        value = value - piece
    return pieces


def frequencies():
    exponent = jnp.arange(0, HEAD_SIZE, 2).astype(jnp.float32) / HEAD_SIZE
    return jnp.power(rope_theta, -exponent)


def rotate(vectors, angles):
    half_size = vectors.shape[-1] // 2
    first_half = vectors[..., :half_size]
    second_half = vectors[..., half_size:]
    cosine_table = jnp.cos(angles)
    sine_table = jnp.sin(angles)
    return jnp.concatenate(
        [
            first_half * cosine_table - second_half * sine_table,
            second_half * cosine_table + first_half * sine_table,
        ],
        -1,
    )


def local(
    token_input_state,
    query_matrix,
    key_value_weight,
    output_weight,
    key_cache_rows,
    value_cache_rows,
    live_lengths,
    owner_shard,
):
    batch_rows = token_input_state.shape[0]
    kv_local = key_cache_rows.shape[1]
    slot_count = key_cache_rows.shape[2]
    row_count = query_matrix.shape[0]
    shard_index = lax.axis_index(SEQ)
    shard_total = lax.axis_size(SEQ)
    local_cols = lax.dynamic_slice_in_dim(token_input_state, shard_index * row_count, row_count, 1)
    query_part = jnp.dot(local_cols, query_matrix, preferred_element_type=jnp.float32)
    keyval_part = jnp.dot(local_cols, key_value_weight, preferred_element_type=jnp.float32)
    parts = jnp.concatenate(
        [query_part.reshape(batch_rows, QUERY_GROUP, HEAD_SIZE), keyval_part.reshape(batch_rows, 2, HEAD_SIZE)], 1
    ).reshape(batch_rows * (QUERY_GROUP + 2), HEAD_SIZE)
    parts = copies_from(parts, SEQ[1:]).sum(0)
    parts = exchanges(parts, SEQ[0]).reshape(batch_rows, 1, QUERY_GROUP + 2, HEAD_SIZE)
    query_rows = parts[:, :, :QUERY_GROUP]
    key_value_rows = parts[:, :, QUERY_GROUP:]
    columns = jnp.arange(shard_total)[None, :]
    lookup = jnp.sum(jnp.where(columns == owner_shard[:, None], live_lengths, 0), 1)
    own_length = jnp.sum(jnp.where(columns == shard_index, live_lengths, 0), 1)
    position = owner_shard * slot_count + lookup
    angles = position.astype(jnp.float32)[:, None] * frequencies()[None, :]
    query_rot = rotate(query_rows, angles[:, None, None, :]).astype(jnp.bfloat16)
    key_new = rotate(key_value_rows[:, :, 0], angles[:, None, :]).astype(jnp.bfloat16)
    value_new = key_value_rows[:, :, 1].astype(jnp.bfloat16)
    scaling = 1.0 / math.sqrt(HEAD_SIZE)
    new_score = (
        jnp.sum(query_rot.astype(jnp.float32) * key_new.astype(jnp.float32)[:, :, None, :], -1)
        * scaling
    )
    is_owner = (owner_shard == shard_index)[:, None, None]
    start_top = jnp.where(is_owner, new_score, -jnp.inf)
    scores = (
        jnp.einsum("bhgd,bhld->bhgl", query_rot, key_cache_rows, preferred_element_type=jnp.float32)
        * scaling
    )
    live_mask = jnp.arange(slot_count)[None, :] < own_length[:, None]
    scores = jnp.where(live_mask[:, None, None, :], scores, -jnp.inf)
    shard_top = jnp.maximum(jnp.max(scores, -1), start_top)
    prob_block = jnp.exp(scores - shard_top[..., None]).astype(jnp.bfloat16)
    totals = jnp.sum(prob_block, -1, dtype=jnp.float32)
    accum = jnp.einsum(
        "bhgl,bhld->bhgd", prob_block, value_cache_rows, preferred_element_type=jnp.float32
    )
    new_prob = jnp.where(is_owner, jnp.exp(new_score - shard_top), 0.0).astype(jnp.bfloat16)
    totals = totals + new_prob.astype(jnp.float32)
    accum = (
        accum
        + new_prob.astype(jnp.float32)[..., None] * value_new.astype(jnp.float32)[:, :, None, :]
    )
    rows = batch_rows * QUERY_GROUP
    aux = jnp.stack(split(shard_top.reshape(rows), 3) + split(totals.reshape(rows), 2))
    aux = jnp.pad(aux, ((0, 3), (0, HEAD_SIZE - rows)))
    message = jnp.concatenate([accum.reshape(rows, HEAD_SIZE).astype(jnp.bfloat16), aux])
    got = copies_from(message, SEQ)
    aux = got[:, rows:, :rows].astype(jnp.float32)
    tops = aux[:, 0] + aux[:, 1] + aux[:, 2]
    weights = jnp.exp(tops - jnp.max(tops, 0))
    totals = jnp.sum(weights * (aux[:, 3] + aux[:, 4]), 0)
    accum = jnp.sum(weights[..., None] * got[:, :rows].astype(jnp.float32), 0)
    attended = (
        (accum / totals[..., None]).astype(jnp.bfloat16).reshape(batch_rows, rows // batch_rows * HEAD_SIZE)
    )
    partial_value = jnp.dot(attended, output_weight, preferred_element_type=jnp.float32)
    other = lax.ppermute(partial_value, "kv", ((0, 1), (1, 0)))
    return (partial_value + other).astype(jnp.bfloat16)


def solution(mesh):
    finer = Mesh(
        mesh.devices.reshape(mesh.shape["kv"], 4, 4, 4, mesh.shape["dp"]),
        ("kv", "seq_0", "seq_1", "seq_2", "dp"),
    )
    return jax.shard_map(
        local,
        mesh=finer,
        in_specs=(
            P("dp", None),
            P(SEQ, "kv"),
            P(SEQ, "kv"),
            P("kv", SEQ),
            P("dp", "kv", SEQ, None),
            P("dp", "kv", SEQ, None),
            P("dp", None),
            P("dp"),
        ),
        out_specs=P("dp", SEQ),
        check_vma=False,
    )
```

```python
import math

import jax
import jax.numpy as jnp
from jax import lax
from jax.experimental import pallas as pl
from jax.experimental.pallas import tpu as pltpu
from jax.sharding import Mesh
from jax.sharding import PartitionSpec as P

HEAD_SIZE = 128
QUERY_GROUP = 8
SEQ = ("seq_0", "seq_1", "seq_2")


rope_theta = 500000.0


def exchanges(array, axis):
    beside = lax.ppermute(array, axis, ((0, 1), (1, 0), (2, 3), (3, 2)))
    around = lax.ppermute(array, axis, ((0, 3), (3, 0), (1, 2), (2, 1)))
    across = lax.ppermute(array, axis, ((0, 2), (2, 0), (1, 3), (3, 1)))
    return beside, around, across


def held(array):
    return pltpu.with_memory_space_constraint(array, pltpu.VMEM)


def left(array):
    return pltpu.with_memory_space_constraint(array, pltpu.HBM)


def vmem():
    return pl.BlockSpec(memory_space=pltpu.VMEM)


def hbm():
    return pl.BlockSpec(memory_space=pltpu.HBM)


def smem():
    return pl.BlockSpec(memory_space=pltpu.SMEM)


def project_kernel(shard_ref, state_ref, query_ref, keyval_ref, out_ref, state_v, query_v, keyval_v, sems):
    columns = pl.ds(pl.multiple_of(shard_ref[0] * query_v.shape[0], query_v.shape[0]), query_v.shape[0])
    loads = [
        pltpu.make_async_copy(query_ref, query_v, sems.at[0]),
        pltpu.make_async_copy(keyval_ref, keyval_v, sems.at[1]),
        pltpu.make_async_copy(state_ref.at[:, columns], state_v, sems.at[2]),
    ]
    for load in loads:
        load.start()
    for load in loads:
        load.wait()
    state = state_v[...]
    parts = []
    for weights in (query_v, keyval_v):
        product = jnp.dot(state, weights[...], preferred_element_type=jnp.float32)
        parts += [product[:, at : at + HEAD_SIZE] for at in range(0, product.shape[1], HEAD_SIZE)]
    rows = jnp.concatenate(parts, 0)
    for copy in range(out_ref.shape[0]):
        out_ref[copy] = rows


def load_kernel(key_ref, value_ref, key_out, value_out, sems):
    loads = [
        pltpu.make_async_copy(key_ref, key_out, sems.at[0]),
        pltpu.make_async_copy(value_ref, value_out, sems.at[1]),
    ]
    for load in loads:
        load.start()
    for load in loads:
        load.wait()


def attend_kernel(
    length_ref, owner_ref, own_ref, beside_ref, around_ref, across_ref, cosine_ref, sine_ref,
    key_ref, value_ref, out_ref, score_ref,
):
    total = (own_ref[...] + beside_ref[...]) + (around_ref[...] + across_ref[...])
    turned = total * cosine_ref[...] + pltpu.roll(total, HEAD_SIZE // 2, 1) * sine_ref[...]
    score_ref[0 : total.shape[0], 0:HEAD_SIZE] = turned
    batch, _, slots, _ = key_ref.shape
    scaling = 1.0 / math.sqrt(HEAD_SIZE)
    lane = lax.broadcasted_iota(jnp.int32, (QUERY_GROUP, HEAD_SIZE), 1)
    sublane = lax.broadcasted_iota(jnp.int32, (QUERY_GROUP, HEAD_SIZE), 0)
    top_row = jnp.zeros((1, HEAD_SIZE), jnp.float32)
    total_row = jnp.zeros((1, HEAD_SIZE), jnp.float32)
    picks = []
    for b in range(batch):
        query = score_ref[pl.ds(b, QUERY_GROUP, stride=batch), 0:HEAD_SIZE].astype(jnp.bfloat16)
        key_new = turned[QUERY_GROUP * batch + b :][:1].astype(jnp.bfloat16)
        value_new = turned[(QUERY_GROUP + 1) * batch + b :][:1].astype(jnp.bfloat16)
        picks.append((query, key_new.astype(jnp.float32), value_new.astype(jnp.float32)))
    slot = lax.broadcasted_iota(jnp.int32, (QUERY_GROUP, slots), 1)
    accums = []
    for b, (query, key_new, value_new) in enumerate(picks):
        scores = (
            lax.dot_general(
                query, key_ref[b, 0], (((1,), (1,)), ((), ())), preferred_element_type=jnp.float32
            )
            * scaling
        )
        scores = jnp.where(slot < length_ref[b], scores, -jnp.inf)
        new_score = jnp.sum(query.astype(jnp.float32) * key_new, -1, keepdims=True) * scaling
        owns = owner_ref[b] > 0
        top = jnp.maximum(jnp.max(scores, -1, keepdims=True), jnp.where(owns, new_score, -jnp.inf))
        prob = jnp.exp(scores - top).astype(jnp.bfloat16)
        new_prob = jnp.where(owns, jnp.exp(new_score - top), 0.0).astype(jnp.bfloat16).astype(jnp.float32)
        weight = jnp.sum(prob.astype(jnp.float32), -1, keepdims=True) + new_prob
        accum = jnp.dot(prob, value_ref[b, 0], preferred_element_type=jnp.float32) + new_prob * value_new
        accums.append(accum)
        mine = lane == sublane + b * QUERY_GROUP
        top_row += jnp.sum(jnp.where(mine, top, 0.0), 0, keepdims=True)
        total_row += jnp.sum(jnp.where(mine, weight, 0.0), 0, keepdims=True)
    side = jnp.zeros((QUERY_GROUP, HEAD_SIZE), jnp.float32)
    at = 0
    for row, count in ((top_row, 3), (total_row, 2)):
        for _ in range(count):
            piece = row.astype(jnp.bfloat16).astype(jnp.float32)
            side = jnp.where(sublane == at, piece, side)
            row = row - piece
            at += 1
    message = jnp.concatenate(accums + [side], 0).astype(jnp.bfloat16)
    for copy in range(out_ref.shape[0]):
        out_ref[copy] = message


def frequencies():
    exponent = jnp.arange(0, HEAD_SIZE, 2).astype(jnp.float32) / HEAD_SIZE
    return jnp.power(rope_theta, -exponent)


def local(
    token_input_state,
    query_matrix,
    key_value_weight,
    output_weight,
    key_cache_rows,
    value_cache_rows,
    live_lengths,
    owner_shard,
):
    batch_rows = token_input_state.shape[0]
    slot_count = key_cache_rows.shape[2]
    row_count = query_matrix.shape[0]
    shard_index = lax.axis_index(SEQ)
    shard_total = lax.axis_size(SEQ)
    heads = QUERY_GROUP + 2
    rows = batch_rows * heads
    copies = pl.pallas_call(
        project_kernel,
        out_shape=pltpu.VMEM((lax.axis_size(SEQ[1:]), rows, HEAD_SIZE), jnp.float32),
        in_specs=[smem(), hbm(), hbm(), hbm()],
        out_specs=vmem(),
        scratch_shapes=[
            pltpu.VMEM((batch_rows, row_count), jnp.bfloat16),
            pltpu.VMEM(query_matrix.shape, jnp.bfloat16),
            pltpu.VMEM(key_value_weight.shape, jnp.bfloat16),
            pltpu.SemaphoreType.DMA((3,)),
        ],
        compiler_params=pltpu.CompilerParams(vmem_limit_bytes=8 << 20),
        name="project",
    )(shard_index.reshape(1), left(token_input_state), left(query_matrix), left(key_value_weight))
    parts = lax.all_to_all(copies, SEQ[1:], 0, 0, tiled=True).sum(0)
    beside, around, across = exchanges(parts, SEQ[0])
    columns = jnp.arange(shard_total)[None, :]
    lookup = jnp.sum(jnp.where(columns == owner_shard[:, None], live_lengths, 0), 1)
    own_length = jnp.sum(jnp.where(columns == shard_index, live_lengths, 0), 1)
    position = owner_shard * slot_count + lookup
    angles = position.astype(jnp.float32)[:, None] * frequencies()[None, :]
    cosine, sine = jnp.cos(angles), jnp.sin(angles)
    one, zero = jnp.ones_like(angles), jnp.zeros_like(angles)
    cosine = jnp.concatenate([cosine, cosine], 1)
    sine = jnp.concatenate([-sine, sine], 1)
    straight = jnp.concatenate([one, one], 1)
    cosine = jnp.concatenate([cosine] * (heads - 1) + [straight], 0)
    sine = jnp.concatenate([sine] * (heads - 1) + [jnp.zeros_like(straight)], 0)
    is_owner = (owner_shard == shard_index).astype(jnp.int32)
    count = batch_rows * QUERY_GROUP
    keys, values = pl.pallas_call(
        load_kernel,
        out_shape=[pltpu.VMEM(a.shape, a.dtype) for a in (key_cache_rows, value_cache_rows)],
        in_specs=[hbm(), hbm()],
        out_specs=[vmem(), vmem()],
        scratch_shapes=[pltpu.SemaphoreType.DMA((2,))],
        compiler_params=pltpu.CompilerParams(vmem_limit_bytes=8 << 20),
        name="load",
    )(left(key_cache_rows), left(value_cache_rows))
    message = pl.pallas_call(
        attend_kernel,
        out_shape=pltpu.VMEM((shard_total, count + QUERY_GROUP, HEAD_SIZE), jnp.bfloat16),
        in_specs=[smem(), smem()] + [vmem()] * 8,
        out_specs=vmem(),
        scratch_shapes=[pltpu.VMEM((rows, HEAD_SIZE), jnp.float32)],
        compiler_params=pltpu.CompilerParams(vmem_limit_bytes=8 << 20),
        name="attend",
    )(
        own_length,
        is_owner,
        *(held(a) for a in (parts, beside, around, across, cosine, sine, keys, values)),
    )
    got = lax.all_to_all(message, SEQ, 0, 0, tiled=True)
    aux = got[:, count:, :count].astype(jnp.float32)
    tops = aux[:, 0] + aux[:, 1] + aux[:, 2]
    weights = jnp.exp(tops - jnp.max(tops, 0))
    totals = jnp.sum(weights * (aux[:, 3] + aux[:, 4]), 0)
    accum = jnp.sum(weights[..., None] * got[:, :count].astype(jnp.float32), 0)
    attended = (accum / totals[..., None]).astype(jnp.bfloat16).reshape(batch_rows, QUERY_GROUP * HEAD_SIZE)
    partial_value = jnp.dot(attended, output_weight, preferred_element_type=jnp.float32)
    other = lax.ppermute(partial_value, "kv", ((0, 1), (1, 0)))
    return (partial_value + other).astype(jnp.bfloat16)


def solution(mesh):
    finer = Mesh(
        mesh.devices.reshape(mesh.shape["kv"], 4, 4, 4, mesh.shape["dp"]),
        ("kv", "seq_0", "seq_1", "seq_2", "dp"),
    )
    return jax.shard_map(
        local,
        mesh=finer,
        in_specs=(
            P("dp", None),
            P(SEQ, "kv"),
            P(SEQ, "kv"),
            P("kv", SEQ),
            P("dp", "kv", SEQ, None),
            P("dp", "kv", SEQ, None),
            P("dp", None),
            P("dp"),
        ),
        out_specs=P("dp", SEQ),
        check_vma=False,
    )
```

```python
import math

import jax
import jax.numpy as jnp
from jax import lax
from jax.experimental import pallas as pl
from jax.experimental.pallas import tpu as pltpu
from jax.sharding import Mesh
from jax.sharding import PartitionSpec as P

HEAD_SIZE = 128
QUERY_GROUP = 8
SEQ = ("seq_0", "seq_1", "seq_2")


rope_theta = 500000.0


def exchanges(array, axis):
    beside = lax.ppermute(array, axis, ((0, 1), (1, 0), (2, 3), (3, 2)))
    around = lax.ppermute(array, axis, ((0, 3), (3, 0), (1, 2), (2, 1)))
    across = lax.ppermute(array, axis, ((0, 2), (2, 0), (1, 3), (3, 1)))
    return beside, around, across


def held(array):
    return pltpu.with_memory_space_constraint(array, pltpu.VMEM)


def left(array):
    return pltpu.with_memory_space_constraint(array, pltpu.HBM)


def vmem():
    return pl.BlockSpec(memory_space=pltpu.VMEM)


def hbm():
    return pl.BlockSpec(memory_space=pltpu.HBM)


def smem():
    return pl.BlockSpec(memory_space=pltpu.SMEM)


def project_kernel(shard_ref, state_ref, query_ref, keyval_ref, out_ref, state_v, query_v, keyval_v, sems):
    columns = pl.ds(pl.multiple_of(shard_ref[0] * query_v.shape[0], query_v.shape[0]), query_v.shape[0])
    loads = [
        pltpu.make_async_copy(query_ref, query_v, sems.at[0]),
        pltpu.make_async_copy(keyval_ref, keyval_v, sems.at[1]),
        pltpu.make_async_copy(state_ref.at[:, columns], state_v, sems.at[2]),
    ]
    for load in loads:
        load.start()
    for load in loads:
        load.wait()
    state = state_v[...]
    parts = []
    for weights in (query_v, keyval_v):
        product = jnp.dot(state, weights[...], preferred_element_type=jnp.float32)
        parts += [product[:, at : at + HEAD_SIZE] for at in range(0, product.shape[1], HEAD_SIZE)]
    rows = jnp.concatenate(parts, 0)
    for copy in range(out_ref.shape[0]):
        out_ref[copy] = rows


def prepare_kernel(
    shard_ref, live_ref, owner_ref, rate_ref, key_ref, value_ref, output_ref,
    key_out, value_out, output_out, cosine_ref, sine_ref, own_ref, sems,
):
    batch, _, slots, _ = key_ref.shape
    loads = [pltpu.make_async_copy(output_ref, output_out, sems.at[2 * batch])]
    for b in range(batch):
        loads.append(pltpu.make_async_copy(key_ref.at[b], key_out.at[b], sems.at[b]))
        loads.append(pltpu.make_async_copy(value_ref.at[b], value_out.at[b], sems.at[batch + b]))
    for load in loads:
        load.start()
    sublane = lax.broadcasted_iota(jnp.int32, (2 * batch, HEAD_SIZE), 0)
    lane = lax.broadcasted_iota(jnp.int32, (2 * batch, HEAD_SIZE), 1)
    place = jnp.zeros((2 * batch, HEAD_SIZE), jnp.int32)
    own = place
    for b in range(batch):
        position = owner_ref[b] * slots + live_ref[b, owner_ref[b]]
        place = jnp.where(sublane % batch == b, position, place)
        own = jnp.where(sublane == b, live_ref[b, shard_ref[0]], own)
        own = jnp.where(sublane == b + batch, jnp.where(owner_ref[b] == shard_ref[0], 1, 0), own)
    own_ref[...] = own
    angle = place.astype(jnp.float32) * rate_ref[...]
    cosine_ref[...] = jnp.cos(angle)
    sine = jnp.sin(angle)
    sine_ref[...] = jnp.where(lane < HEAD_SIZE // 2, -sine, sine)
    for load in loads:
        load.wait()


def attend_kernel(
    part_ref, beside_ref, around_ref, across_ref, cosine_ref, sine_ref, own_ref,
    key_ref, value_ref, out_ref, score_ref,
):
    batch, _, slots, _ = key_ref.shape
    cosine, sine = cosine_ref[...], sine_ref[...]
    straight = lax.broadcasted_iota(jnp.int32, cosine.shape, 0) >= batch
    for at in range(0, score_ref.shape[0], 2 * batch):
        tile = pl.ds(at, 2 * batch)
        total = (part_ref[tile, :] + beside_ref[tile, :]) + (around_ref[tile, :] + across_ref[tile, :])
        if at + 2 * batch == score_ref.shape[0]:
            cosine = jnp.where(straight, 1.0, cosine)
            sine = jnp.where(straight, 0.0, sine)
        turned = total * cosine + pltpu.roll(total, HEAD_SIZE // 2, 1) * sine
        score_ref[tile, :] = turned
    scaling = 1.0 / math.sqrt(HEAD_SIZE)
    lane = lax.broadcasted_iota(jnp.int32, (QUERY_GROUP, HEAD_SIZE), 1)
    sublane = lax.broadcasted_iota(jnp.int32, (QUERY_GROUP, HEAD_SIZE), 0)
    top_row = jnp.zeros((1, HEAD_SIZE), jnp.float32)
    total_row = jnp.zeros((1, HEAD_SIZE), jnp.float32)
    picks = []
    for b in range(batch):
        query = score_ref[pl.ds(b, QUERY_GROUP, stride=batch), :].astype(jnp.bfloat16)
        key_new = turned[b : b + 1].astype(jnp.bfloat16)
        value_new = turned[batch + b : batch + b + 1].astype(jnp.bfloat16)
        picks.append((query, key_new.astype(jnp.float32), value_new.astype(jnp.float32)))
    slot = lax.broadcasted_iota(jnp.int32, (QUERY_GROUP, slots), 1)
    accums = []
    for b, (query, key_new, value_new) in enumerate(picks):
        scores = (
            lax.dot_general(
                query, key_ref[b, 0], (((1,), (1,)), ((), ())), preferred_element_type=jnp.float32
            )
            * scaling
        )
        scores = jnp.where(slot < own_ref[b : b + 1, 0:1], scores, -jnp.inf)
        new_score = jnp.sum(query.astype(jnp.float32) * key_new, -1, keepdims=True) * scaling
        owns = own_ref[batch + b : batch + b + 1, 0:1] > 0
        top = jnp.maximum(jnp.max(scores, -1, keepdims=True), jnp.where(owns, new_score, -jnp.inf))
        prob = jnp.exp(scores - top).astype(jnp.bfloat16)
        new_prob = jnp.where(owns, jnp.exp(new_score - top), 0.0).astype(jnp.bfloat16).astype(jnp.float32)
        weight = jnp.sum(prob.astype(jnp.float32), -1, keepdims=True) + new_prob
        accum = jnp.dot(prob, value_ref[b, 0], preferred_element_type=jnp.float32) + new_prob * value_new
        accums.append(accum)
        mine = lane == sublane + b * QUERY_GROUP
        top_row += jnp.sum(jnp.where(mine, top, 0.0), 0, keepdims=True)
        total_row += jnp.sum(jnp.where(mine, weight, 0.0), 0, keepdims=True)
    side = jnp.zeros((QUERY_GROUP, HEAD_SIZE), jnp.float32)
    at = 0
    for row, count in ((top_row, 3), (total_row, 2)):
        for _ in range(count):
            piece = row.astype(jnp.bfloat16).astype(jnp.float32)
            side = jnp.where(sublane == at, piece, side)
            row = row - piece
            at += 1
    message = jnp.concatenate(accums + [side], 0).astype(jnp.bfloat16)
    for copy in range(out_ref.shape[0]):
        out_ref[copy] = message


def merge_kernel(got_ref, output_ref, out_ref):
    sources = got_ref.shape[0]
    batch = out_ref.shape[0]
    count = batch * QUERY_GROUP
    side = got_ref[:, count:, :].astype(jnp.float32).reshape(sources * QUERY_GROUP, HEAD_SIZE).astype(jnp.bfloat16)
    source = lax.broadcasted_iota(jnp.int32, (HEAD_SIZE, sources * QUERY_GROUP), 0)
    entry = lax.broadcasted_iota(jnp.int32, (HEAD_SIZE, sources * QUERY_GROUP), 1)
    place = entry - source * QUERY_GROUP

    def gathered(low, high):
        chosen = ((place >= low) & (place < high)).astype(jnp.float32).astype(jnp.bfloat16)
        return jnp.dot(chosen, side, preferred_element_type=jnp.float32).T[:count]

    there = lax.broadcasted_iota(jnp.int32, (count, HEAD_SIZE), 1) < sources
    tops = jnp.where(there, gathered(0, 3), -jnp.inf)
    weights = jnp.exp(tops - jnp.max(tops, -1, keepdims=True))
    total = jnp.sum(weights * gathered(3, 5), -1, keepdims=True)
    accum = jnp.zeros((count, HEAD_SIZE), jnp.float32)
    for at in range(sources):
        accum += weights[:, at : at + 1] * got_ref[at, :count, :].astype(jnp.float32)
    attended = accum / total
    head = lax.broadcasted_iota(jnp.int32, (count, HEAD_SIZE), 0) % QUERY_GROUP
    spread = jnp.concatenate(
        [jnp.where(head == at, attended, 0.0).astype(jnp.bfloat16) for at in range(QUERY_GROUP)], 1
    )
    product = jnp.dot(spread, output_ref[...], preferred_element_type=jnp.float32)
    out_ref[...] = jnp.sum(product.reshape(batch, QUERY_GROUP, HEAD_SIZE), 1)


def merge_kernel(got_ref, output_ref, out_ref):
    sources = got_ref.shape[0]
    batch = out_ref.shape[0]
    count = batch * QUERY_GROUP
    side = got_ref[:, count:, :].astype(jnp.float32).reshape(sources * QUERY_GROUP, HEAD_SIZE).astype(jnp.bfloat16)
    source = lax.broadcasted_iota(jnp.int32, (HEAD_SIZE, sources * QUERY_GROUP), 0)
    entry = lax.broadcasted_iota(jnp.int32, (HEAD_SIZE, sources * QUERY_GROUP), 1)
    place = entry - source * QUERY_GROUP

    def gathered(low, high):
        chosen = ((place >= low) & (place < high)).astype(jnp.float32).astype(jnp.bfloat16)
        return jnp.dot(chosen, side, preferred_element_type=jnp.float32).T[:count]

    there = lax.broadcasted_iota(jnp.int32, (count, HEAD_SIZE), 1) < sources
    tops = jnp.where(there, gathered(0, 3), -jnp.inf)
    weights = jnp.exp(tops - jnp.max(tops, -1, keepdims=True))
    total = jnp.sum(weights * gathered(3, 5), -1, keepdims=True)
    accum = jnp.zeros((count, HEAD_SIZE), jnp.float32)
    for at in range(sources):
        accum += weights[:, at : at + 1] * got_ref[at, :count, :].astype(jnp.float32)
    attended = accum / total
    head = lax.broadcasted_iota(jnp.int32, (count, HEAD_SIZE), 0) % QUERY_GROUP
    spread = jnp.concatenate(
        [jnp.where(head == at, attended, 0.0).astype(jnp.bfloat16) for at in range(QUERY_GROUP)], 1
    )
    product = jnp.dot(spread, output_ref[...], preferred_element_type=jnp.float32)
    out_ref[...] = jnp.sum(product.reshape(batch, QUERY_GROUP, HEAD_SIZE), 1)


def frequencies():
    exponent = jnp.arange(0, HEAD_SIZE, 2).astype(jnp.float32) / HEAD_SIZE
    return jnp.power(rope_theta, -exponent)


def local(
    token_input_state,
    query_matrix,
    key_value_weight,
    output_weight,
    key_cache_rows,
    value_cache_rows,
    live_lengths,
    owner_shard,
):
    batch_rows = token_input_state.shape[0]
    row_count = query_matrix.shape[0]
    shard_index = lax.axis_index(SEQ)
    heads = QUERY_GROUP + 2
    rows = batch_rows * heads
    exponent = jnp.arange(0, HEAD_SIZE, 2).astype(jnp.float32) / HEAD_SIZE
    rates = jnp.power(rope_theta, -exponent)
    rates = jnp.concatenate([rates, rates]).reshape(1, HEAD_SIZE)
    index, rates = lax.optimization_barrier((shard_index.reshape(1), rates))
    copies = pl.pallas_call(
        project_kernel,
        out_shape=pltpu.VMEM((lax.axis_size(SEQ[1:]), rows, HEAD_SIZE), jnp.float32),
        in_specs=[smem(), hbm(), hbm(), hbm()],
        out_specs=vmem(),
        scratch_shapes=[
            pltpu.VMEM((batch_rows, row_count), jnp.bfloat16),
            pltpu.VMEM(query_matrix.shape, jnp.bfloat16),
            pltpu.VMEM(key_value_weight.shape, jnp.bfloat16),
            pltpu.SemaphoreType.DMA((3,)),
        ],
        compiler_params=pltpu.CompilerParams(vmem_limit_bytes=8 << 20),
        name="project",
    )(index, left(token_input_state), left(query_matrix), left(key_value_weight))
    got = lax.all_to_all(copies, SEQ[1:], 0, 0, tiled=True)
    got, later_index, rates = lax.optimization_barrier((got, index, rates))
    parts = got.sum(0)
    beside, around, across = exchanges(parts, SEQ[0])
    caches = (key_cache_rows, value_cache_rows, output_weight)
    table = pltpu.VMEM((2 * batch_rows, HEAD_SIZE), jnp.float32)
    places = pltpu.VMEM((2 * batch_rows, HEAD_SIZE), jnp.int32)
    keys, values, outputs, cosine, sine, own = pl.pallas_call(
        prepare_kernel,
        out_shape=[*(pltpu.VMEM(a.shape, a.dtype) for a in caches), table, table, places],
        in_specs=[smem()] * 3 + [vmem()] + [hbm()] * 3,
        out_specs=[vmem()] * 6,
        scratch_shapes=[pltpu.SemaphoreType.DMA((2 * batch_rows + 1,))],
        compiler_params=pltpu.CompilerParams(vmem_limit_bytes=8 << 20),
        name="prepare",
    )(
        later_index,
        left(live_lengths),
        left(owner_shard),
        rates,
        *(left(a) for a in caches),
    )
    count = batch_rows * QUERY_GROUP
    message = pl.pallas_call(
        attend_kernel,
        out_shape=pltpu.VMEM((lax.axis_size(SEQ), count + QUERY_GROUP, HEAD_SIZE), jnp.bfloat16),
        in_specs=[vmem()] * 9,
        out_specs=vmem(),
        scratch_shapes=[pltpu.VMEM((rows, HEAD_SIZE), jnp.float32)],
        compiler_params=pltpu.CompilerParams(vmem_limit_bytes=8 << 20),
        name="attend",
    )(
        *(held(a) for a in (parts, beside, around, across, cosine, sine, own, keys, values)),
    )
    got = lax.all_to_all(message, SEQ, 0, 0, tiled=True)
    partial_value = pl.pallas_call(
        merge_kernel,
        out_shape=pltpu.VMEM((batch_rows, HEAD_SIZE), jnp.float32),
        in_specs=[vmem()] * 2,
        out_specs=vmem(),
        compiler_params=pltpu.CompilerParams(vmem_limit_bytes=8 << 20),
        name="merge",
    )(held(got), held(outputs))
    other = lax.ppermute(partial_value, "kv", ((0, 1), (1, 0)))
    return (partial_value + other).astype(jnp.bfloat16)


def solution(mesh):
    finer = Mesh(
        mesh.devices.reshape(mesh.shape["kv"], 4, 4, 4, mesh.shape["dp"]),
        ("kv", "seq_0", "seq_1", "seq_2", "dp"),
    )
    return jax.shard_map(
        local,
        mesh=finer,
        in_specs=(
            P("dp", None),
            P(SEQ, "kv"),
            P(SEQ, "kv"),
            P("kv", SEQ),
            P("dp", "kv", SEQ, None),
            P("dp", "kv", SEQ, None),
            P("dp", None),
            P("dp"),
        ),
        out_specs=P("dp", SEQ),
        check_vma=False,
    )
```

```python
import math

import jax
import jax.numpy as jnp
from jax import lax
from jax.experimental import pallas as pl
from jax.experimental.pallas import tpu as pltpu
from jax.sharding import Mesh
from jax.sharding import PartitionSpec as P

HEAD_SIZE = 128
QUERY_GROUP = 8
SEQ = ("seq_0", "seq_1", "seq_2")


rope_theta = 500000.0


def exchanges(array, axis):
    beside = lax.ppermute(array, axis, ((0, 1), (1, 0), (2, 3), (3, 2)))
    around = lax.ppermute(array, axis, ((0, 3), (3, 0), (1, 2), (2, 1)))
    across = lax.ppermute(array, axis, ((0, 2), (2, 0), (1, 3), (3, 1)))
    return beside, around, across


def held(array):
    return pltpu.with_memory_space_constraint(array, pltpu.VMEM)


def left(array):
    return pltpu.with_memory_space_constraint(array, pltpu.HBM)


def vmem():
    return pl.BlockSpec(memory_space=pltpu.VMEM)


def hbm():
    return pl.BlockSpec(memory_space=pltpu.HBM)


def smem():
    return pl.BlockSpec(memory_space=pltpu.SMEM)


def project_kernel(shard_ref, state_ref, query_ref, keyval_ref, out_ref, state_v, query_v, keyval_v, sems):
    columns = pl.ds(pl.multiple_of(shard_ref[0] * query_v.shape[0], query_v.shape[0]), query_v.shape[0])
    loads = [
        pltpu.make_async_copy(query_ref, query_v, sems.at[0]),
        pltpu.make_async_copy(keyval_ref, keyval_v, sems.at[1]),
        pltpu.make_async_copy(state_ref.at[:, columns], state_v, sems.at[2]),
    ]
    for load in loads:
        load.start()
    for load in loads:
        load.wait()
    state = state_v[...]
    parts = []
    for weights in (query_v, keyval_v):
        product = jnp.dot(state, weights[...], preferred_element_type=jnp.float32)
        parts += [product[:, at : at + HEAD_SIZE] for at in range(0, product.shape[1], HEAD_SIZE)]
    rows = jnp.concatenate(parts, 0)
    for copy in range(out_ref.shape[0]):
        out_ref[copy] = rows


def prepare_kernel(
    shard_ref, live_ref, owner_ref, rate_ref, key_ref, value_ref, output_ref,
    key_out, value_out, output_out, cosine_ref, sine_ref, own_ref, sems,
):
    batch, _, slots, _ = key_ref.shape
    loads = [pltpu.make_async_copy(output_ref, output_out, sems.at[2 * batch])]
    for b in range(batch):
        loads.append(pltpu.make_async_copy(key_ref.at[b], key_out.at[b], sems.at[b]))
        loads.append(pltpu.make_async_copy(value_ref.at[b], value_out.at[b], sems.at[batch + b]))
    for load in loads:
        load.start()
    sublane = lax.broadcasted_iota(jnp.int32, (2 * batch, HEAD_SIZE), 0)
    lane = lax.broadcasted_iota(jnp.int32, (2 * batch, HEAD_SIZE), 1)
    place = jnp.zeros((2 * batch, HEAD_SIZE), jnp.int32)
    own = place
    for b in range(batch):
        position = owner_ref[b] * slots + live_ref[b, owner_ref[b]]
        place = jnp.where(sublane % batch == b, position, place)
        own = jnp.where(sublane == b, live_ref[b, shard_ref[0]], own)
        own = jnp.where(sublane == b + batch, jnp.where(owner_ref[b] == shard_ref[0], 1, 0), own)
    own_ref[...] = own
    angle = place.astype(jnp.float32) * rate_ref[...]
    cosine_ref[...] = jnp.cos(angle)
    sine = jnp.sin(angle)
    sine_ref[...] = jnp.where(lane < HEAD_SIZE // 2, -sine, sine)
    for load in loads:
        load.wait()


def attend_kernel(
    part_ref, beside_ref, around_ref, across_ref, cosine_ref, sine_ref, own_ref,
    key_ref, value_ref, out_ref, score_ref,
):
    batch, _, slots, _ = key_ref.shape
    cosine, sine = cosine_ref[...], sine_ref[...]
    straight = lax.broadcasted_iota(jnp.int32, cosine.shape, 0) >= batch
    for at in range(0, score_ref.shape[0], 2 * batch):
        tile = pl.ds(at, 2 * batch)
        total = (part_ref[tile, :] + beside_ref[tile, :]) + (around_ref[tile, :] + across_ref[tile, :])
        if at + 2 * batch == score_ref.shape[0]:
            cosine = jnp.where(straight, 1.0, cosine)
            sine = jnp.where(straight, 0.0, sine)
        turned = total * cosine + pltpu.roll(total, HEAD_SIZE // 2, 1) * sine
        score_ref[tile, :] = turned
    scaling = 1.0 / math.sqrt(HEAD_SIZE)
    lane = lax.broadcasted_iota(jnp.int32, (QUERY_GROUP, HEAD_SIZE), 1)
    sublane = lax.broadcasted_iota(jnp.int32, (QUERY_GROUP, HEAD_SIZE), 0)
    top_row = jnp.zeros((1, HEAD_SIZE), jnp.float32)
    total_row = jnp.zeros((1, HEAD_SIZE), jnp.float32)
    picks = []
    for b in range(batch):
        query = score_ref[pl.ds(b, QUERY_GROUP, stride=batch), :].astype(jnp.bfloat16)
        key_new = turned[b : b + 1].astype(jnp.bfloat16)
        value_new = turned[batch + b : batch + b + 1].astype(jnp.bfloat16)
        picks.append((query, key_new.astype(jnp.float32), value_new.astype(jnp.float32)))
    slot = lax.broadcasted_iota(jnp.int32, (QUERY_GROUP, slots), 1)
    scores_of = [
        lax.dot_general(query, key_ref[b, 0], (((1,), (1,)), ((), ())), preferred_element_type=jnp.float32)
        * scaling
        for b, (query, _, _) in enumerate(picks)
    ]
    probs, additions = [], []
    for b, (query, key_new, value_new) in enumerate(picks):
        scores = jnp.where(slot < own_ref[b : b + 1, 0:1], scores_of[b], -jnp.inf)
        new_score = jnp.sum(query.astype(jnp.float32) * key_new, -1, keepdims=True) * scaling
        owns = own_ref[batch + b : batch + b + 1, 0:1] > 0
        top = jnp.maximum(jnp.max(scores, -1, keepdims=True), jnp.where(owns, new_score, -jnp.inf))
        prob = jnp.exp(scores - top).astype(jnp.bfloat16)
        new_prob = jnp.where(owns, jnp.exp(new_score - top), 0.0).astype(jnp.bfloat16).astype(jnp.float32)
        weight = jnp.sum(prob.astype(jnp.float32), -1, keepdims=True) + new_prob
        probs.append(prob)
        additions.append(new_prob * value_new)
        mine = lane == sublane + b * QUERY_GROUP
        top_row += jnp.sum(jnp.where(mine, top, 0.0), 0, keepdims=True)
        total_row += jnp.sum(jnp.where(mine, weight, 0.0), 0, keepdims=True)
    accums = [
        jnp.dot(prob, value_ref[b, 0], preferred_element_type=jnp.float32) + additions[b]
        for b, prob in enumerate(probs)
    ]
    side = jnp.zeros((QUERY_GROUP, HEAD_SIZE), jnp.float32)
    at = 0
    for row, count in ((top_row, 3), (total_row, 2)):
        for _ in range(count):
            piece = row.astype(jnp.bfloat16).astype(jnp.float32)
            side = jnp.where(sublane == at, piece, side)
            row = row - piece
            at += 1
    message = jnp.concatenate(accums + [side], 0).astype(jnp.bfloat16)
    for copy in range(out_ref.shape[0]):
        out_ref[copy] = message


def merge_kernel(got_ref, output_ref, out_ref):
    sources = got_ref.shape[0]
    batch = out_ref.shape[0]
    count = batch * QUERY_GROUP
    side = got_ref[:, count:, :].astype(jnp.float32).reshape(sources * QUERY_GROUP, HEAD_SIZE).astype(jnp.bfloat16)
    source = lax.broadcasted_iota(jnp.int32, (2 * sources, sources * QUERY_GROUP), 0)
    entry = lax.broadcasted_iota(jnp.int32, (2 * sources, sources * QUERY_GROUP), 1)
    place = entry - source * QUERY_GROUP
    of_total = place + sources * QUERY_GROUP
    chosen = ((place >= 0) & (place < 3)) | ((of_total >= 3) & (of_total < 5))
    chosen = chosen.astype(jnp.float32).astype(jnp.bfloat16)
    found = jnp.dot(chosen, side, preferred_element_type=jnp.float32).T[:count]
    tops, totals = found[:, :sources], found[:, sources:]
    weights = jnp.exp(tops - jnp.max(tops, -1, keepdims=True))
    total = jnp.sum(weights * totals, -1, keepdims=True)
    accum = jnp.zeros((count, HEAD_SIZE), jnp.float32)
    for at in range(sources):
        accum += weights[:, at : at + 1] * got_ref[at, :count, :].astype(jnp.float32)
    attended = accum / total
    head = lax.broadcasted_iota(jnp.int32, (count, HEAD_SIZE), 0) % QUERY_GROUP
    spread = jnp.concatenate(
        [jnp.where(head == at, attended, 0.0).astype(jnp.bfloat16) for at in range(QUERY_GROUP)], 1
    )
    product = jnp.dot(spread, output_ref[...], preferred_element_type=jnp.float32)
    out_ref[...] = jnp.sum(product.reshape(batch, QUERY_GROUP, HEAD_SIZE), 1)


def merge_kernel(got_ref, output_ref, out_ref):
    sources = got_ref.shape[0]
    batch = out_ref.shape[0]
    count = batch * QUERY_GROUP
    side = got_ref[:, count:, :].astype(jnp.float32).reshape(sources * QUERY_GROUP, HEAD_SIZE).astype(jnp.bfloat16)
    source = lax.broadcasted_iota(jnp.int32, (HEAD_SIZE, sources * QUERY_GROUP), 0)
    entry = lax.broadcasted_iota(jnp.int32, (HEAD_SIZE, sources * QUERY_GROUP), 1)
    place = entry - source * QUERY_GROUP

    def gathered(low, high):
        chosen = ((place >= low) & (place < high)).astype(jnp.float32).astype(jnp.bfloat16)
        return jnp.dot(chosen, side, preferred_element_type=jnp.float32).T[:count]

    there = lax.broadcasted_iota(jnp.int32, (count, HEAD_SIZE), 1) < sources
    tops = jnp.where(there, gathered(0, 3), -jnp.inf)
    weights = jnp.exp(tops - jnp.max(tops, -1, keepdims=True))
    total = jnp.sum(weights * gathered(3, 5), -1, keepdims=True)
    accum = jnp.zeros((count, HEAD_SIZE), jnp.float32)
    for at in range(sources):
        accum += weights[:, at : at + 1] * got_ref[at, :count, :].astype(jnp.float32)
    attended = accum / total
    head = lax.broadcasted_iota(jnp.int32, (count, HEAD_SIZE), 0) % QUERY_GROUP
    spread = jnp.concatenate(
        [jnp.where(head == at, attended, 0.0).astype(jnp.bfloat16) for at in range(QUERY_GROUP)], 1
    )
    product = jnp.dot(spread, output_ref[...], preferred_element_type=jnp.float32)
    out_ref[...] = jnp.sum(product.reshape(batch, QUERY_GROUP, HEAD_SIZE), 1)


def frequencies():
    exponent = jnp.arange(0, HEAD_SIZE, 2).astype(jnp.float32) / HEAD_SIZE
    return jnp.power(rope_theta, -exponent)


def local(
    token_input_state,
    query_matrix,
    key_value_weight,
    output_weight,
    key_cache_rows,
    value_cache_rows,
    live_lengths,
    owner_shard,
):
    batch_rows = token_input_state.shape[0]
    row_count = query_matrix.shape[0]
    shard_index = lax.axis_index(SEQ)
    heads = QUERY_GROUP + 2
    rows = batch_rows * heads
    exponent = jnp.arange(0, HEAD_SIZE, 2).astype(jnp.float32) / HEAD_SIZE
    rates = jnp.power(rope_theta, -exponent)
    rates = jnp.concatenate([rates, rates]).reshape(1, HEAD_SIZE)
    index, rates = lax.optimization_barrier((shard_index.reshape(1), rates))
    copies = pl.pallas_call(
        project_kernel,
        out_shape=pltpu.VMEM((lax.axis_size(SEQ[1:]), rows, HEAD_SIZE), jnp.float32),
        in_specs=[smem(), hbm(), hbm(), hbm()],
        out_specs=vmem(),
        scratch_shapes=[
            pltpu.VMEM((batch_rows, row_count), jnp.bfloat16),
            pltpu.VMEM(query_matrix.shape, jnp.bfloat16),
            pltpu.VMEM(key_value_weight.shape, jnp.bfloat16),
            pltpu.SemaphoreType.DMA((3,)),
        ],
        compiler_params=pltpu.CompilerParams(vmem_limit_bytes=8 << 20),
        name="project",
    )(index, left(token_input_state), left(query_matrix), left(key_value_weight))
    got = lax.all_to_all(copies, SEQ[1:], 0, 0, tiled=True)
    got, later_index, rates = lax.optimization_barrier((got, index, rates))
    parts = got.sum(0)
    beside, around, across = exchanges(parts, SEQ[0])
    caches = (key_cache_rows, value_cache_rows, output_weight)
    table = pltpu.VMEM((2 * batch_rows, HEAD_SIZE), jnp.float32)
    places = pltpu.VMEM((2 * batch_rows, HEAD_SIZE), jnp.int32)
    keys, values, outputs, cosine, sine, own = pl.pallas_call(
        prepare_kernel,
        out_shape=[*(pltpu.VMEM(a.shape, a.dtype) for a in caches), table, table, places],
        in_specs=[smem()] * 3 + [vmem()] + [hbm()] * 3,
        out_specs=[vmem()] * 6,
        scratch_shapes=[pltpu.SemaphoreType.DMA((2 * batch_rows + 1,))],
        compiler_params=pltpu.CompilerParams(vmem_limit_bytes=8 << 20),
        name="prepare",
    )(
        later_index,
        left(live_lengths),
        left(owner_shard),
        rates,
        *(left(a) for a in caches),
    )
    count = batch_rows * QUERY_GROUP
    message = pl.pallas_call(
        attend_kernel,
        out_shape=pltpu.VMEM((lax.axis_size(SEQ), count + QUERY_GROUP, HEAD_SIZE), jnp.bfloat16),
        in_specs=[vmem()] * 9,
        out_specs=vmem(),
        scratch_shapes=[pltpu.VMEM((rows, HEAD_SIZE), jnp.float32)],
        compiler_params=pltpu.CompilerParams(vmem_limit_bytes=8 << 20),
        name="attend",
    )(
        *(held(a) for a in (parts, beside, around, across, cosine, sine, own, keys, values)),
    )
    got = lax.all_to_all(message, SEQ, 0, 0, tiled=True)
    partial_value = pl.pallas_call(
        merge_kernel,
        out_shape=pltpu.VMEM((batch_rows, HEAD_SIZE), jnp.float32),
        in_specs=[vmem()] * 2,
        out_specs=vmem(),
        compiler_params=pltpu.CompilerParams(vmem_limit_bytes=8 << 20),
        name="merge",
    )(held(got), held(outputs))
    other = lax.ppermute(partial_value, "kv", ((0, 1), (1, 0)))
    return (partial_value + other).astype(jnp.bfloat16)


def solution(mesh):
    finer = Mesh(
        mesh.devices.reshape(mesh.shape["kv"], 4, 4, 4, mesh.shape["dp"]),
        ("kv", "seq_0", "seq_1", "seq_2", "dp"),
    )
    return jax.shard_map(
        local,
        mesh=finer,
        in_specs=(
            P("dp", None),
            P(SEQ, "kv"),
            P(SEQ, "kv"),
            P("kv", SEQ),
            P("dp", "kv", SEQ, None),
            P("dp", "kv", SEQ, None),
            P("dp", None),
            P("dp"),
        ),
        out_specs=P("dp", SEQ),
        check_vma=False,
    )
```

```python
import math

import jax
import jax.numpy as jnp
from jax import lax
from jax.experimental import pallas as pl
from jax.experimental.pallas import tpu as pltpu
from jax.sharding import Mesh
from jax.sharding import PartitionSpec as P

HEAD_SIZE = 128
QUERY_GROUP = 8
SEQ = ("seq_0", "seq_1", "seq_2")


rope_theta = 500000.0


def exchanges(array, axis):
    beside = lax.ppermute(array, axis, ((0, 1), (1, 2), (2, 3), (3, 0)))
    around = lax.ppermute(array, axis, ((0, 3), (1, 0), (2, 1), (3, 2)))
    across = lax.ppermute(array, axis, ((0, 2), (2, 0), (1, 3), (3, 1)))
    return beside, around, across


def held(array):
    return pltpu.with_memory_space_constraint(array, pltpu.VMEM)


def left(array):
    return pltpu.with_memory_space_constraint(array, pltpu.HBM)


def vmem():
    return pl.BlockSpec(memory_space=pltpu.VMEM)


def hbm():
    return pl.BlockSpec(memory_space=pltpu.HBM)


def smem():
    return pl.BlockSpec(memory_space=pltpu.SMEM)


def project_kernel(shard_ref, state_ref, query_ref, keyval_ref, out_ref, state_v, query_v, keyval_v, sems):
    columns = pl.ds(pl.multiple_of(shard_ref[0] * query_v.shape[0], query_v.shape[0]), query_v.shape[0])
    loads = [
        pltpu.make_async_copy(query_ref, query_v, sems.at[0]),
        pltpu.make_async_copy(keyval_ref, keyval_v, sems.at[1]),
        pltpu.make_async_copy(state_ref.at[:, columns], state_v, sems.at[2]),
    ]
    for load in loads:
        load.start()
    for load in loads:
        load.wait()
    state = state_v[...]
    parts = []
    for weights in (query_v, keyval_v):
        product = jnp.dot(state, weights[...], preferred_element_type=jnp.float32)
        parts += [product[:, at : at + HEAD_SIZE] for at in range(0, product.shape[1], HEAD_SIZE)]
    rows = jnp.concatenate(parts, 0)
    for copy in range(out_ref.shape[0]):
        out_ref[copy] = rows


def prepare_kernel(
    shard_ref, live_ref, owner_ref, rate_ref, key_ref, value_ref, output_ref,
    key_out, value_out, output_out, cosine_ref, sine_ref, own_ref, sems,
):
    batch, _, slots, _ = key_ref.shape
    loads = [pltpu.make_async_copy(output_ref, output_out, sems.at[2 * batch])]
    for b in range(batch):
        loads.append(pltpu.make_async_copy(key_ref.at[b], key_out.at[b], sems.at[b]))
        loads.append(pltpu.make_async_copy(value_ref.at[b], value_out.at[b], sems.at[batch + b]))
    for load in loads:
        load.start()
    sublane = lax.broadcasted_iota(jnp.int32, (2 * batch, HEAD_SIZE), 0)
    lane = lax.broadcasted_iota(jnp.int32, (2 * batch, HEAD_SIZE), 1)
    place = jnp.zeros((2 * batch, HEAD_SIZE), jnp.int32)
    own = place
    for b in range(batch):
        position = owner_ref[b] * slots + live_ref[b, owner_ref[b]]
        place = jnp.where(sublane % batch == b, position, place)
        own = jnp.where(sublane == b, live_ref[b, shard_ref[0]], own)
        own = jnp.where(sublane == b + batch, jnp.where(owner_ref[b] == shard_ref[0], 1, 0), own)
    own_ref[...] = own
    angle = place.astype(jnp.float32) * rate_ref[...]
    cosine_ref[...] = jnp.cos(angle)
    sine = jnp.sin(angle)
    sine_ref[...] = jnp.where(lane < HEAD_SIZE // 2, -sine, sine)
    for load in loads:
        load.wait()


def attend_kernel(
    part_ref, beside_ref, around_ref, across_ref, cosine_ref, sine_ref, own_ref,
    key_ref, value_ref, out_ref, score_ref,
):
    batch, _, slots, _ = key_ref.shape
    cosine, sine = cosine_ref[...], sine_ref[...]
    straight = lax.broadcasted_iota(jnp.int32, cosine.shape, 0) >= batch
    for at in range(0, score_ref.shape[0], 2 * batch):
        tile = pl.ds(at, 2 * batch)
        total = (part_ref[tile, :] + across_ref[tile, :]) + (beside_ref[tile, :] + around_ref[tile, :])
        if at + 2 * batch == score_ref.shape[0]:
            cosine = jnp.where(straight, 1.0, cosine)
            sine = jnp.where(straight, 0.0, sine)
        turned = total * cosine + pltpu.roll(total, HEAD_SIZE // 2, 1) * sine
        score_ref[tile, :] = turned
    scaling = 1.0 / math.sqrt(HEAD_SIZE)
    lane = lax.broadcasted_iota(jnp.int32, (QUERY_GROUP, HEAD_SIZE), 1)
    sublane = lax.broadcasted_iota(jnp.int32, (QUERY_GROUP, HEAD_SIZE), 0)
    top_row = jnp.zeros((1, HEAD_SIZE), jnp.float32)
    total_row = jnp.zeros((1, HEAD_SIZE), jnp.float32)
    picks = []
    for b in range(batch):
        query = score_ref[pl.ds(b, QUERY_GROUP, stride=batch), :].astype(jnp.bfloat16)
        key_new = turned[b : b + 1].astype(jnp.bfloat16)
        value_new = turned[batch + b : batch + b + 1].astype(jnp.bfloat16)
        picks.append((query, key_new.astype(jnp.float32), value_new.astype(jnp.float32)))
    slot = lax.broadcasted_iota(jnp.int32, (QUERY_GROUP, slots), 1)
    scores_of = [
        lax.dot_general(query, key_ref[b, 0], (((1,), (1,)), ((), ())), preferred_element_type=jnp.float32)
        * scaling
        for b, (query, _, _) in enumerate(picks)
    ]
    probs, additions = [], []
    for b, (query, key_new, value_new) in enumerate(picks):
        scores = jnp.where(slot < own_ref[b : b + 1, 0:1], scores_of[b], -jnp.inf)
        new_score = jnp.sum(query.astype(jnp.float32) * key_new, -1, keepdims=True) * scaling
        owns = own_ref[batch + b : batch + b + 1, 0:1] > 0
        top = jnp.maximum(jnp.max(scores, -1, keepdims=True), jnp.where(owns, new_score, -jnp.inf))
        prob = jnp.exp(scores - top).astype(jnp.bfloat16)
        new_prob = jnp.where(owns, jnp.exp(new_score - top), 0.0).astype(jnp.bfloat16).astype(jnp.float32)
        weight = jnp.sum(prob.astype(jnp.float32), -1, keepdims=True) + new_prob
        probs.append(prob)
        additions.append(new_prob * value_new)
        mine = lane == sublane + b * QUERY_GROUP
        top_row += jnp.sum(jnp.where(mine, top, 0.0), 0, keepdims=True)
        total_row += jnp.sum(jnp.where(mine, weight, 0.0), 0, keepdims=True)
    accums = [
        jnp.dot(prob, value_ref[b, 0], preferred_element_type=jnp.float32) + additions[b]
        for b, prob in enumerate(probs)
    ]
    side = jnp.zeros((QUERY_GROUP, HEAD_SIZE), jnp.float32)
    at = 0
    for row, count in ((top_row, 3), (total_row, 2)):
        for _ in range(count):
            piece = row.astype(jnp.bfloat16).astype(jnp.float32)
            side = jnp.where(sublane == at, piece, side)
            row = row - piece
            at += 1
    message = jnp.concatenate(accums + [side], 0).astype(jnp.bfloat16)
    for copy in range(out_ref.shape[0]):
        out_ref[copy] = message


def merge_kernel(got_ref, output_ref, out_ref):
    sources = got_ref.shape[0]
    batch = out_ref.shape[0]
    count = batch * QUERY_GROUP
    side = got_ref[:, count:, :].astype(jnp.float32).reshape(sources * QUERY_GROUP, HEAD_SIZE).astype(jnp.bfloat16)
    source = lax.broadcasted_iota(jnp.int32, (2 * sources, sources * QUERY_GROUP), 0)
    entry = lax.broadcasted_iota(jnp.int32, (2 * sources, sources * QUERY_GROUP), 1)
    place = entry - source * QUERY_GROUP
    of_total = place + sources * QUERY_GROUP
    chosen = ((place >= 0) & (place < 3)) | ((of_total >= 3) & (of_total < 5))
    chosen = chosen.astype(jnp.float32).astype(jnp.bfloat16)
    found = jnp.dot(chosen, side, preferred_element_type=jnp.float32).T[:count]
    tops, totals = found[:, :sources], found[:, sources:]
    weights = jnp.exp(tops - jnp.max(tops, -1, keepdims=True))
    total = jnp.sum(weights * totals, -1, keepdims=True)
    accum = jnp.zeros((count, HEAD_SIZE), jnp.float32)
    for at in range(sources):
        accum += weights[:, at : at + 1] * got_ref[at, :count, :].astype(jnp.float32)
    attended = accum / total
    head = lax.broadcasted_iota(jnp.int32, (count, HEAD_SIZE), 0) % QUERY_GROUP
    spread = jnp.concatenate(
        [jnp.where(head == at, attended, 0.0).astype(jnp.bfloat16) for at in range(QUERY_GROUP)], 1
    )
    product = jnp.dot(spread, output_ref[...], preferred_element_type=jnp.float32)
    out_ref[...] = jnp.sum(product.reshape(batch, QUERY_GROUP, HEAD_SIZE), 1)


def merge_kernel(got_ref, output_ref, out_ref):
    sources = got_ref.shape[0]
    batch = out_ref.shape[0]
    count = batch * QUERY_GROUP
    side = got_ref[:, count:, :].astype(jnp.float32).reshape(sources * QUERY_GROUP, HEAD_SIZE).astype(jnp.bfloat16)
    source = lax.broadcasted_iota(jnp.int32, (HEAD_SIZE, sources * QUERY_GROUP), 0)
    entry = lax.broadcasted_iota(jnp.int32, (HEAD_SIZE, sources * QUERY_GROUP), 1)
    place = entry - source * QUERY_GROUP

    def gathered(low, high):
        chosen = ((place >= low) & (place < high)).astype(jnp.float32).astype(jnp.bfloat16)
        return jnp.dot(chosen, side, preferred_element_type=jnp.float32).T[:count]

    there = lax.broadcasted_iota(jnp.int32, (count, HEAD_SIZE), 1) < sources
    tops = jnp.where(there, gathered(0, 3), -jnp.inf)
    weights = jnp.exp(tops - jnp.max(tops, -1, keepdims=True))
    total = jnp.sum(weights * gathered(3, 5), -1, keepdims=True)
    accum = jnp.zeros((count, HEAD_SIZE), jnp.float32)
    for at in range(sources):
        accum += weights[:, at : at + 1] * got_ref[at, :count, :].astype(jnp.float32)
    attended = accum / total
    head = lax.broadcasted_iota(jnp.int32, (count, HEAD_SIZE), 0) % QUERY_GROUP
    spread = jnp.concatenate(
        [jnp.where(head == at, attended, 0.0).astype(jnp.bfloat16) for at in range(QUERY_GROUP)], 1
    )
    product = jnp.dot(spread, output_ref[...], preferred_element_type=jnp.float32)
    out_ref[...] = jnp.sum(product.reshape(batch, QUERY_GROUP, HEAD_SIZE), 1)


def frequencies():
    exponent = jnp.arange(0, HEAD_SIZE, 2).astype(jnp.float32) / HEAD_SIZE
    return jnp.power(rope_theta, -exponent)


def local(
    token_input_state,
    query_matrix,
    key_value_weight,
    output_weight,
    key_cache_rows,
    value_cache_rows,
    live_lengths,
    owner_shard,
):
    batch_rows = token_input_state.shape[0]
    row_count = query_matrix.shape[0]
    shard_index = lax.axis_index(SEQ)
    heads = QUERY_GROUP + 2
    rows = batch_rows * heads
    exponent = jnp.arange(0, HEAD_SIZE, 2).astype(jnp.float32) / HEAD_SIZE
    rates = jnp.power(rope_theta, -exponent)
    rates = jnp.concatenate([rates, rates]).reshape(1, HEAD_SIZE)
    index, rates = lax.optimization_barrier((shard_index.reshape(1), rates))
    copies = pl.pallas_call(
        project_kernel,
        out_shape=pltpu.VMEM((lax.axis_size(SEQ[1:]), rows, HEAD_SIZE), jnp.float32),
        in_specs=[smem(), hbm(), hbm(), hbm()],
        out_specs=vmem(),
        scratch_shapes=[
            pltpu.VMEM((batch_rows, row_count), jnp.bfloat16),
            pltpu.VMEM(query_matrix.shape, jnp.bfloat16),
            pltpu.VMEM(key_value_weight.shape, jnp.bfloat16),
            pltpu.SemaphoreType.DMA((3,)),
        ],
        compiler_params=pltpu.CompilerParams(vmem_limit_bytes=8 << 20),
        name="project",
    )(index, left(token_input_state), left(query_matrix), left(key_value_weight))
    got = lax.all_to_all(copies, SEQ[1:], 0, 0, tiled=True)
    got, later_index, rates = lax.optimization_barrier((got, index, rates))
    parts = got.sum(0)
    beside, around, across = exchanges(parts, SEQ[0])
    caches = (key_cache_rows, value_cache_rows, output_weight)
    table = pltpu.VMEM((2 * batch_rows, HEAD_SIZE), jnp.float32)
    places = pltpu.VMEM((2 * batch_rows, HEAD_SIZE), jnp.int32)
    keys, values, outputs, cosine, sine, own = pl.pallas_call(
        prepare_kernel,
        out_shape=[*(pltpu.VMEM(a.shape, a.dtype) for a in caches), table, table, places],
        in_specs=[smem()] * 3 + [vmem()] + [hbm()] * 3,
        out_specs=[vmem()] * 6,
        scratch_shapes=[pltpu.SemaphoreType.DMA((2 * batch_rows + 1,))],
        compiler_params=pltpu.CompilerParams(vmem_limit_bytes=8 << 20),
        name="prepare",
    )(
        later_index,
        left(live_lengths),
        left(owner_shard),
        rates,
        *(left(a) for a in caches),
    )
    count = batch_rows * QUERY_GROUP
    message = pl.pallas_call(
        attend_kernel,
        out_shape=pltpu.VMEM((lax.axis_size(SEQ), count + QUERY_GROUP, HEAD_SIZE), jnp.bfloat16),
        in_specs=[vmem()] * 9,
        out_specs=vmem(),
        scratch_shapes=[pltpu.VMEM((rows, HEAD_SIZE), jnp.float32)],
        compiler_params=pltpu.CompilerParams(vmem_limit_bytes=8 << 20),
        name="attend",
    )(
        *(held(a) for a in (parts, beside, around, across, cosine, sine, own, keys, values)),
    )
    got = lax.all_to_all(message, SEQ, 0, 0, tiled=True)
    partial_value = pl.pallas_call(
        merge_kernel,
        out_shape=pltpu.VMEM((batch_rows, HEAD_SIZE), jnp.float32),
        in_specs=[vmem()] * 2,
        out_specs=vmem(),
        compiler_params=pltpu.CompilerParams(vmem_limit_bytes=8 << 20),
        name="merge",
    )(held(got), held(outputs))
    other = lax.ppermute(partial_value, "kv", ((0, 1), (1, 0)))
    return (partial_value + other).astype(jnp.bfloat16)


def solution(mesh):
    finer = Mesh(
        mesh.devices.reshape(mesh.shape["kv"], 4, 4, 4, mesh.shape["dp"]),
        ("kv", "seq_0", "seq_1", "seq_2", "dp"),
    )
    return jax.shard_map(
        local,
        mesh=finer,
        in_specs=(
            P("dp", None),
            P(SEQ, "kv"),
            P(SEQ, "kv"),
            P("kv", SEQ),
            P("dp", "kv", SEQ, None),
            P("dp", "kv", SEQ, None),
            P("dp", None),
            P("dp"),
        ),
        out_specs=P("dp", SEQ),
        check_vma=False,
    )
```

```python
import math

import jax
import jax.numpy as jnp
from jax import lax
from jax.experimental import pallas as pl
from jax.experimental.pallas import tpu as pltpu
from jax.sharding import Mesh
from jax.sharding import PartitionSpec as P

HEAD_SIZE = 128
QUERY_GROUP = 8
SEQ = ("seq_0", "seq_1", "seq_2")
MIXED = (
    29, 28, 24, 33, 35, 60, 23, 40, 11, 27, 61, 3, 5, 7, 42, 45,
    12, 59, 0, 55, 1, 44, 41, 14, 15, 17, 47, 20, 63, 10, 62, 54,
    36, 51, 21, 4, 43, 52, 9, 38, 34, 58, 39, 6, 46, 18, 8, 57,
    13, 37, 22, 30, 19, 53, 50, 25, 31, 32, 16, 2, 26, 56, 48, 49,
)


rope_theta = 500000.0


def exchanges(array, axis):
    beside = lax.ppermute(array, axis, ((0, 1), (1, 2), (2, 3), (3, 0)))
    around = lax.ppermute(array, axis, ((0, 3), (1, 0), (2, 1), (3, 2)))
    across = lax.ppermute(array, axis, ((0, 2), (2, 0), (1, 3), (3, 1)))
    return beside, around, across


def held(array):
    return pltpu.with_memory_space_constraint(array, pltpu.VMEM)


def left(array):
    return pltpu.with_memory_space_constraint(array, pltpu.HBM)


def vmem():
    return pl.BlockSpec(memory_space=pltpu.VMEM)


def hbm():
    return pl.BlockSpec(memory_space=pltpu.HBM)


def smem():
    return pl.BlockSpec(memory_space=pltpu.SMEM)


def project_kernel(shard_ref, state_ref, query_ref, keyval_ref, out_ref, state_v, query_v, keyval_v, sems):
    columns = pl.ds(pl.multiple_of(shard_ref[0] * query_v.shape[0], query_v.shape[0]), query_v.shape[0])
    loads = [
        pltpu.make_async_copy(query_ref, query_v, sems.at[0]),
        pltpu.make_async_copy(keyval_ref, keyval_v, sems.at[1]),
        pltpu.make_async_copy(state_ref.at[:, columns], state_v, sems.at[2]),
    ]
    for load in loads:
        load.start()
    for load in loads:
        load.wait()
    state = state_v[...]
    parts = []
    for weights in (query_v, keyval_v):
        product = jnp.dot(state, weights[...], preferred_element_type=jnp.float32)
        parts += [product[:, at : at + HEAD_SIZE] for at in range(0, product.shape[1], HEAD_SIZE)]
    rows = jnp.concatenate(parts, 0)
    for copy in range(out_ref.shape[0]):
        out_ref[copy] = rows


def prepare_kernel(
    shard_ref, live_ref, owner_ref, rate_ref, key_ref, value_ref, output_ref,
    key_out, value_out, output_out, cosine_ref, sine_ref, own_ref, sems,
):
    batch, _, slots, _ = key_ref.shape
    loads = [pltpu.make_async_copy(output_ref, output_out, sems.at[2 * batch])]
    for b in range(batch):
        loads.append(pltpu.make_async_copy(key_ref.at[b], key_out.at[b], sems.at[b]))
        loads.append(pltpu.make_async_copy(value_ref.at[b], value_out.at[b], sems.at[batch + b]))
    for load in loads:
        load.start()
    sublane = lax.broadcasted_iota(jnp.int32, (2 * batch, HEAD_SIZE), 0)
    lane = lax.broadcasted_iota(jnp.int32, (2 * batch, HEAD_SIZE), 1)
    place = jnp.zeros((2 * batch, HEAD_SIZE), jnp.int32)
    own = place
    for b in range(batch):
        position = owner_ref[b] * slots + live_ref[b, owner_ref[b]]
        place = jnp.where(sublane % batch == b, position, place)
        own = jnp.where(sublane == b, live_ref[b, shard_ref[0]], own)
        own = jnp.where(sublane == b + batch, jnp.where(owner_ref[b] == shard_ref[0], 1, 0), own)
    own_ref[...] = own
    angle = place.astype(jnp.float32) * rate_ref[...]
    cosine_ref[...] = jnp.cos(angle)
    sine = jnp.sin(angle)
    sine_ref[...] = jnp.where(lane < HEAD_SIZE // 2, -sine, sine)
    for load in loads:
        load.wait()


def attend_kernel(
    part_ref, beside_ref, around_ref, across_ref, cosine_ref, sine_ref, own_ref,
    key_ref, value_ref, out_ref, score_ref,
):
    batch, _, slots, _ = key_ref.shape
    cosine, sine = cosine_ref[...], sine_ref[...]
    straight = lax.broadcasted_iota(jnp.int32, cosine.shape, 0) >= batch
    for at in range(0, score_ref.shape[0], 2 * batch):
        tile = pl.ds(at, 2 * batch)
        total = (part_ref[tile, :] + across_ref[tile, :]) + (beside_ref[tile, :] + around_ref[tile, :])
        if at + 2 * batch == score_ref.shape[0]:
            cosine = jnp.where(straight, 1.0, cosine)
            sine = jnp.where(straight, 0.0, sine)
        turned = total * cosine + pltpu.roll(total, HEAD_SIZE // 2, 1) * sine
        score_ref[tile, :] = turned
    scaling = 1.0 / math.sqrt(HEAD_SIZE)
    lane = lax.broadcasted_iota(jnp.int32, (QUERY_GROUP, HEAD_SIZE), 1)
    sublane = lax.broadcasted_iota(jnp.int32, (QUERY_GROUP, HEAD_SIZE), 0)
    top_row = jnp.zeros((1, HEAD_SIZE), jnp.float32)
    total_row = jnp.zeros((1, HEAD_SIZE), jnp.float32)
    picks = []
    for b in range(batch):
        query = score_ref[pl.ds(b, QUERY_GROUP, stride=batch), :].astype(jnp.bfloat16)
        key_new = turned[b : b + 1].astype(jnp.bfloat16)
        value_new = turned[batch + b : batch + b + 1].astype(jnp.bfloat16)
        picks.append((query, key_new.astype(jnp.float32), value_new.astype(jnp.float32)))
    slot = lax.broadcasted_iota(jnp.int32, (QUERY_GROUP, slots), 1)
    scores_of = [
        lax.dot_general(query, key_ref[b, 0], (((1,), (1,)), ((), ())), preferred_element_type=jnp.float32)
        * scaling
        for b, (query, _, _) in enumerate(picks)
    ]
    probs, additions = [], []
    for b, (query, key_new, value_new) in enumerate(picks):
        scores = jnp.where(slot < own_ref[b : b + 1, 0:1], scores_of[b], -jnp.inf)
        new_score = jnp.sum(query.astype(jnp.float32) * key_new, -1, keepdims=True) * scaling
        owns = own_ref[batch + b : batch + b + 1, 0:1] > 0
        top = jnp.maximum(jnp.max(scores, -1, keepdims=True), jnp.where(owns, new_score, -jnp.inf))
        prob = jnp.exp(scores - top).astype(jnp.bfloat16)
        new_prob = jnp.where(owns, jnp.exp(new_score - top), 0.0).astype(jnp.bfloat16).astype(jnp.float32)
        weight = jnp.sum(prob.astype(jnp.float32), -1, keepdims=True) + new_prob
        probs.append(prob)
        additions.append(new_prob * value_new)
        mine = lane == sublane + b * QUERY_GROUP
        top_row += jnp.sum(jnp.where(mine, top, 0.0), 0, keepdims=True)
        total_row += jnp.sum(jnp.where(mine, weight, 0.0), 0, keepdims=True)
    accums = [
        jnp.dot(prob, value_ref[b, 0], preferred_element_type=jnp.float32) + additions[b]
        for b, prob in enumerate(probs)
    ]
    side = jnp.zeros((QUERY_GROUP, HEAD_SIZE), jnp.float32)
    at = 0
    for row, count in ((top_row, 3), (total_row, 2)):
        for _ in range(count):
            piece = row.astype(jnp.bfloat16).astype(jnp.float32)
            side = jnp.where(sublane == at, piece, side)
            row = row - piece
            at += 1
    message = jnp.concatenate(accums + [side], 0).astype(jnp.bfloat16)
    for copy in range(out_ref.shape[0]):
        out_ref[copy] = message


def merge_kernel(got_ref, output_ref, out_ref):
    sources = got_ref.shape[0]
    batch = out_ref.shape[0]
    count = batch * QUERY_GROUP
    side = got_ref[:, count:, :].astype(jnp.float32).reshape(sources * QUERY_GROUP, HEAD_SIZE).astype(jnp.bfloat16)
    source = lax.broadcasted_iota(jnp.int32, (2 * sources, sources * QUERY_GROUP), 0)
    entry = lax.broadcasted_iota(jnp.int32, (2 * sources, sources * QUERY_GROUP), 1)
    place = entry - source * QUERY_GROUP
    of_total = place + sources * QUERY_GROUP
    chosen = ((place >= 0) & (place < 3)) | ((of_total >= 3) & (of_total < 5))
    chosen = chosen.astype(jnp.float32).astype(jnp.bfloat16)
    found = jnp.dot(chosen, side, preferred_element_type=jnp.float32).T[:count]
    tops, totals = found[:, :sources], found[:, sources:]
    weights = jnp.exp(tops - jnp.max(tops, -1, keepdims=True))
    total = jnp.sum(weights * totals, -1, keepdims=True)
    accum = jnp.zeros((count, HEAD_SIZE), jnp.float32)
    for at in range(sources):
        accum += weights[:, at : at + 1] * got_ref[at, :count, :].astype(jnp.float32)
    attended = accum / total
    head = lax.broadcasted_iota(jnp.int32, (count, HEAD_SIZE), 0) % QUERY_GROUP
    spread = jnp.concatenate(
        [jnp.where(head == at, attended, 0.0).astype(jnp.bfloat16) for at in range(QUERY_GROUP)], 1
    )
    product = jnp.dot(spread, output_ref[...], preferred_element_type=jnp.float32)
    out_ref[...] = jnp.sum(product.reshape(batch, QUERY_GROUP, HEAD_SIZE), 1)


def merge_kernel(got_ref, output_ref, out_ref):
    sources = got_ref.shape[0]
    batch = out_ref.shape[0]
    count = batch * QUERY_GROUP
    side = got_ref[:, count:, :].astype(jnp.float32).reshape(sources * QUERY_GROUP, HEAD_SIZE).astype(jnp.bfloat16)
    source = lax.broadcasted_iota(jnp.int32, (HEAD_SIZE, sources * QUERY_GROUP), 0)
    entry = lax.broadcasted_iota(jnp.int32, (HEAD_SIZE, sources * QUERY_GROUP), 1)
    place = entry - source * QUERY_GROUP

    def gathered(low, high):
        chosen = ((place >= low) & (place < high)).astype(jnp.float32).astype(jnp.bfloat16)
        return jnp.dot(chosen, side, preferred_element_type=jnp.float32).T[:count]

    there = lax.broadcasted_iota(jnp.int32, (count, HEAD_SIZE), 1) < sources
    tops = jnp.where(there, gathered(0, 3), -jnp.inf)
    weights = jnp.exp(tops - jnp.max(tops, -1, keepdims=True))
    total = jnp.sum(weights * gathered(3, 5), -1, keepdims=True)
    accum = jnp.zeros((count, HEAD_SIZE), jnp.float32)
    for at in range(sources):
        accum += weights[:, at : at + 1] * got_ref[at, :count, :].astype(jnp.float32)
    attended = accum / total
    head = lax.broadcasted_iota(jnp.int32, (count, HEAD_SIZE), 0) % QUERY_GROUP
    spread = jnp.concatenate(
        [jnp.where(head == at, attended, 0.0).astype(jnp.bfloat16) for at in range(QUERY_GROUP)], 1
    )
    product = jnp.dot(spread, output_ref[...], preferred_element_type=jnp.float32)
    out_ref[...] = jnp.sum(product.reshape(batch, QUERY_GROUP, HEAD_SIZE), 1)


def frequencies():
    exponent = jnp.arange(0, HEAD_SIZE, 2).astype(jnp.float32) / HEAD_SIZE
    return jnp.power(rope_theta, -exponent)


def local(
    token_input_state,
    query_matrix,
    key_value_weight,
    output_weight,
    key_cache_rows,
    value_cache_rows,
    live_lengths,
    owner_shard,
):
    batch_rows = token_input_state.shape[0]
    row_count = query_matrix.shape[0]
    shard_index = lax.axis_index(SEQ)
    heads = QUERY_GROUP + 2
    rows = batch_rows * heads
    exponent = jnp.arange(0, HEAD_SIZE, 2).astype(jnp.float32) / HEAD_SIZE
    rates = jnp.power(rope_theta, -exponent)
    rates = jnp.concatenate([rates, rates]).reshape(1, HEAD_SIZE)
    index, rates = lax.optimization_barrier((shard_index.reshape(1), rates))
    copies = pl.pallas_call(
        project_kernel,
        out_shape=pltpu.VMEM((lax.axis_size(SEQ[1:]), rows, HEAD_SIZE), jnp.float32),
        in_specs=[smem(), hbm(), hbm(), hbm()],
        out_specs=vmem(),
        scratch_shapes=[
            pltpu.VMEM((batch_rows, row_count), jnp.bfloat16),
            pltpu.VMEM(query_matrix.shape, jnp.bfloat16),
            pltpu.VMEM(key_value_weight.shape, jnp.bfloat16),
            pltpu.SemaphoreType.DMA((3,)),
        ],
        compiler_params=pltpu.CompilerParams(vmem_limit_bytes=8 << 20),
        name="project",
    )(index, left(token_input_state), left(query_matrix), left(key_value_weight))
    got = lax.all_to_all(copies, SEQ[1:], 0, 0, tiled=True)
    got, later_index, rates = lax.optimization_barrier((got, index, rates))
    parts = got.sum(0)
    beside, around, across = exchanges(parts, SEQ[0])
    caches = (key_cache_rows, value_cache_rows, output_weight)
    table = pltpu.VMEM((2 * batch_rows, HEAD_SIZE), jnp.float32)
    places = pltpu.VMEM((2 * batch_rows, HEAD_SIZE), jnp.int32)
    keys, values, outputs, cosine, sine, own = pl.pallas_call(
        prepare_kernel,
        out_shape=[*(pltpu.VMEM(a.shape, a.dtype) for a in caches), table, table, places],
        in_specs=[smem()] * 3 + [vmem()] + [hbm()] * 3,
        out_specs=[vmem()] * 6,
        scratch_shapes=[pltpu.SemaphoreType.DMA((2 * batch_rows + 1,))],
        compiler_params=pltpu.CompilerParams(vmem_limit_bytes=8 << 20),
        name="prepare",
    )(
        later_index,
        left(live_lengths),
        left(owner_shard),
        rates,
        *(left(a) for a in caches),
    )
    count = batch_rows * QUERY_GROUP
    message = pl.pallas_call(
        attend_kernel,
        out_shape=pltpu.VMEM((lax.axis_size(SEQ), count + QUERY_GROUP, HEAD_SIZE), jnp.bfloat16),
        in_specs=[vmem()] * 9,
        out_specs=vmem(),
        scratch_shapes=[pltpu.VMEM((rows, HEAD_SIZE), jnp.float32)],
        compiler_params=pltpu.CompilerParams(vmem_limit_bytes=8 << 20),
        name="attend",
    )(
        *(held(a) for a in (parts, beside, around, across, cosine, sine, own, keys, values)),
    )
    got = lax.all_to_all(message, SEQ, 0, 0, tiled=True, axis_index_groups=[list(MIXED)])
    partial_value = pl.pallas_call(
        merge_kernel,
        out_shape=pltpu.VMEM((batch_rows, HEAD_SIZE), jnp.float32),
        in_specs=[vmem()] * 2,
        out_specs=vmem(),
        compiler_params=pltpu.CompilerParams(vmem_limit_bytes=8 << 20),
        name="merge",
    )(held(got), held(outputs))
    other = lax.ppermute(partial_value, "kv", ((0, 1), (1, 0)))
    return (partial_value + other).astype(jnp.bfloat16)


def solution(mesh):
    finer = Mesh(
        mesh.devices.reshape(mesh.shape["kv"], 4, 4, 4, mesh.shape["dp"]),
        ("kv", "seq_0", "seq_1", "seq_2", "dp"),
    )
    return jax.shard_map(
        local,
        mesh=finer,
        in_specs=(
            P("dp", None),
            P(SEQ, "kv"),
            P(SEQ, "kv"),
            P("kv", SEQ),
            P("dp", "kv", SEQ, None),
            P("dp", "kv", SEQ, None),
            P("dp", None),
            P("dp"),
        ),
        out_specs=P("dp", SEQ),
        check_vma=False,
    )
```

```python
import math

import jax
import jax.numpy as jnp
from jax import lax
from jax.experimental import pallas as pl
from jax.experimental.pallas import tpu as pltpu
from jax.sharding import Mesh
from jax.sharding import PartitionSpec as P

HEAD_SIZE = 128
QUERY_GROUP = 8
SEQ = ("seq_0", "seq_1", "seq_2")
MIXED = (
    29, 28, 24, 33, 35, 60, 23, 40, 11, 27, 61, 3, 5, 7, 42, 45,
    12, 59, 0, 55, 1, 44, 41, 14, 15, 17, 47, 20, 63, 10, 62, 54,
    36, 51, 21, 4, 43, 52, 9, 38, 34, 58, 39, 6, 46, 18, 8, 57,
    13, 37, 22, 30, 19, 53, 50, 25, 31, 32, 16, 2, 26, 56, 48, 49,
)
MIXED_PLANE = (10, 8, 12, 1, 2, 5, 9, 15, 0, 13, 3, 6, 4, 14, 7, 11)


rope_theta = 500000.0


def exchanges(array, axis):
    beside = lax.ppermute(array, axis, ((0, 1), (1, 2), (2, 3), (3, 0)))
    around = lax.ppermute(array, axis, ((0, 3), (1, 0), (2, 1), (3, 2)))
    across = lax.ppermute(array, axis, ((0, 2), (2, 0), (1, 3), (3, 1)))
    return beside, around, across


def held(array):
    return pltpu.with_memory_space_constraint(array, pltpu.VMEM)


def left(array):
    return pltpu.with_memory_space_constraint(array, pltpu.HBM)


def vmem():
    return pl.BlockSpec(memory_space=pltpu.VMEM)


def hbm():
    return pl.BlockSpec(memory_space=pltpu.HBM)


def smem():
    return pl.BlockSpec(memory_space=pltpu.SMEM)


def project_kernel(shard_ref, state_ref, query_ref, keyval_ref, out_ref, state_v, query_v, keyval_v, sems):
    columns = pl.ds(pl.multiple_of(shard_ref[0] * query_v.shape[0], query_v.shape[0]), query_v.shape[0])
    loads = [
        pltpu.make_async_copy(query_ref, query_v, sems.at[0]),
        pltpu.make_async_copy(keyval_ref, keyval_v, sems.at[1]),
        pltpu.make_async_copy(state_ref.at[:, columns], state_v, sems.at[2]),
    ]
    for load in loads:
        load.start()
    for load in loads:
        load.wait()
    state = state_v[...]
    parts = []
    for weights in (query_v, keyval_v):
        product = jnp.dot(state, weights[...], preferred_element_type=jnp.float32)
        parts += [product[:, at : at + HEAD_SIZE] for at in range(0, product.shape[1], HEAD_SIZE)]
    rows = jnp.concatenate(parts, 0)
    for copy in range(out_ref.shape[0]):
        out_ref[copy] = rows


def prepare_kernel(
    shard_ref, live_ref, owner_ref, rate_ref, key_ref, value_ref, output_ref,
    key_out, value_out, output_out, cosine_ref, sine_ref, own_ref, sems,
):
    batch, _, slots, _ = key_ref.shape
    loads = [pltpu.make_async_copy(output_ref, output_out, sems.at[2 * batch])]
    for b in range(batch):
        loads.append(pltpu.make_async_copy(key_ref.at[b], key_out.at[b], sems.at[b]))
        loads.append(pltpu.make_async_copy(value_ref.at[b], value_out.at[b], sems.at[batch + b]))
    for load in loads:
        load.start()
    sublane = lax.broadcasted_iota(jnp.int32, (2 * batch, HEAD_SIZE), 0)
    lane = lax.broadcasted_iota(jnp.int32, (2 * batch, HEAD_SIZE), 1)
    place = jnp.zeros((2 * batch, HEAD_SIZE), jnp.int32)
    own = place
    for b in range(batch):
        position = owner_ref[b] * slots + live_ref[b, owner_ref[b]]
        place = jnp.where(sublane % batch == b, position, place)
        own = jnp.where(sublane == b, live_ref[b, shard_ref[0]], own)
        own = jnp.where(sublane == b + batch, jnp.where(owner_ref[b] == shard_ref[0], 1, 0), own)
    own_ref[...] = own
    angle = place.astype(jnp.float32) * rate_ref[...]
    cosine_ref[...] = jnp.cos(angle)
    sine = jnp.sin(angle)
    sine_ref[...] = jnp.where(lane < HEAD_SIZE // 2, -sine, sine)
    for load in loads:
        load.wait()


def attend_kernel(
    part_ref, beside_ref, around_ref, across_ref, cosine_ref, sine_ref, own_ref,
    key_ref, value_ref, out_ref, score_ref,
):
    batch, _, slots, _ = key_ref.shape
    cosine, sine = cosine_ref[...], sine_ref[...]
    straight = lax.broadcasted_iota(jnp.int32, cosine.shape, 0) >= batch
    for at in range(0, score_ref.shape[0], 2 * batch):
        tile = pl.ds(at, 2 * batch)
        total = (part_ref[tile, :] + across_ref[tile, :]) + (beside_ref[tile, :] + around_ref[tile, :])
        if at + 2 * batch == score_ref.shape[0]:
            cosine = jnp.where(straight, 1.0, cosine)
            sine = jnp.where(straight, 0.0, sine)
        turned = total * cosine + pltpu.roll(total, HEAD_SIZE // 2, 1) * sine
        score_ref[tile, :] = turned
    scaling = 1.0 / math.sqrt(HEAD_SIZE)
    lane = lax.broadcasted_iota(jnp.int32, (QUERY_GROUP, HEAD_SIZE), 1)
    sublane = lax.broadcasted_iota(jnp.int32, (QUERY_GROUP, HEAD_SIZE), 0)
    top_row = jnp.zeros((1, HEAD_SIZE), jnp.float32)
    total_row = jnp.zeros((1, HEAD_SIZE), jnp.float32)
    picks = []
    for b in range(batch):
        query = score_ref[pl.ds(b, QUERY_GROUP, stride=batch), :].astype(jnp.bfloat16)
        key_new = turned[b : b + 1].astype(jnp.bfloat16)
        value_new = turned[batch + b : batch + b + 1].astype(jnp.bfloat16)
        picks.append((query, key_new.astype(jnp.float32), value_new.astype(jnp.float32)))
    slot = lax.broadcasted_iota(jnp.int32, (QUERY_GROUP, slots), 1)
    scores_of = [
        lax.dot_general(query, key_ref[b, 0], (((1,), (1,)), ((), ())), preferred_element_type=jnp.float32)
        * scaling
        for b, (query, _, _) in enumerate(picks)
    ]
    probs, additions = [], []
    for b, (query, key_new, value_new) in enumerate(picks):
        scores = jnp.where(slot < own_ref[b : b + 1, 0:1], scores_of[b], -jnp.inf)
        new_score = jnp.sum(query.astype(jnp.float32) * key_new, -1, keepdims=True) * scaling
        owns = own_ref[batch + b : batch + b + 1, 0:1] > 0
        top = jnp.maximum(jnp.max(scores, -1, keepdims=True), jnp.where(owns, new_score, -jnp.inf))
        prob = jnp.exp(scores - top).astype(jnp.bfloat16)
        new_prob = jnp.where(owns, jnp.exp(new_score - top), 0.0).astype(jnp.bfloat16).astype(jnp.float32)
        weight = jnp.sum(prob.astype(jnp.float32), -1, keepdims=True) + new_prob
        probs.append(prob)
        additions.append(new_prob * value_new)
        mine = lane == sublane + b * QUERY_GROUP
        top_row += jnp.sum(jnp.where(mine, top, 0.0), 0, keepdims=True)
        total_row += jnp.sum(jnp.where(mine, weight, 0.0), 0, keepdims=True)
    accums = [
        jnp.dot(prob, value_ref[b, 0], preferred_element_type=jnp.float32) + additions[b]
        for b, prob in enumerate(probs)
    ]
    side = jnp.zeros((QUERY_GROUP, HEAD_SIZE), jnp.float32)
    at = 0
    for row, count in ((top_row, 3), (total_row, 2)):
        for _ in range(count):
            piece = row.astype(jnp.bfloat16).astype(jnp.float32)
            side = jnp.where(sublane == at, piece, side)
            row = row - piece
            at += 1
    message = jnp.concatenate(accums + [side], 0).astype(jnp.bfloat16)
    for copy in range(out_ref.shape[0]):
        out_ref[copy] = message


def merge_kernel(got_ref, output_ref, out_ref):
    sources = got_ref.shape[0]
    batch = out_ref.shape[0]
    count = batch * QUERY_GROUP
    side = got_ref[:, count:, :].astype(jnp.float32).reshape(sources * QUERY_GROUP, HEAD_SIZE).astype(jnp.bfloat16)
    source = lax.broadcasted_iota(jnp.int32, (2 * sources, sources * QUERY_GROUP), 0)
    entry = lax.broadcasted_iota(jnp.int32, (2 * sources, sources * QUERY_GROUP), 1)
    place = entry - source * QUERY_GROUP
    of_total = place + sources * QUERY_GROUP
    chosen = ((place >= 0) & (place < 3)) | ((of_total >= 3) & (of_total < 5))
    chosen = chosen.astype(jnp.float32).astype(jnp.bfloat16)
    found = jnp.dot(chosen, side, preferred_element_type=jnp.float32).T[:count]
    tops, totals = found[:, :sources], found[:, sources:]
    weights = jnp.exp(tops - jnp.max(tops, -1, keepdims=True))
    total = jnp.sum(weights * totals, -1, keepdims=True)
    accum = jnp.zeros((count, HEAD_SIZE), jnp.float32)
    for at in range(sources):
        accum += weights[:, at : at + 1] * got_ref[at, :count, :].astype(jnp.float32)
    attended = accum / total
    head = lax.broadcasted_iota(jnp.int32, (count, HEAD_SIZE), 0) % QUERY_GROUP
    spread = jnp.concatenate(
        [jnp.where(head == at, attended, 0.0).astype(jnp.bfloat16) for at in range(QUERY_GROUP)], 1
    )
    product = jnp.dot(spread, output_ref[...], preferred_element_type=jnp.float32)
    out_ref[...] = jnp.sum(product.reshape(batch, QUERY_GROUP, HEAD_SIZE), 1)


def merge_kernel(got_ref, output_ref, out_ref):
    sources = got_ref.shape[0]
    batch = out_ref.shape[0]
    count = batch * QUERY_GROUP
    side = got_ref[:, count:, :].astype(jnp.float32).reshape(sources * QUERY_GROUP, HEAD_SIZE).astype(jnp.bfloat16)
    source = lax.broadcasted_iota(jnp.int32, (HEAD_SIZE, sources * QUERY_GROUP), 0)
    entry = lax.broadcasted_iota(jnp.int32, (HEAD_SIZE, sources * QUERY_GROUP), 1)
    place = entry - source * QUERY_GROUP

    def gathered(low, high):
        chosen = ((place >= low) & (place < high)).astype(jnp.float32).astype(jnp.bfloat16)
        return jnp.dot(chosen, side, preferred_element_type=jnp.float32).T[:count]

    there = lax.broadcasted_iota(jnp.int32, (count, HEAD_SIZE), 1) < sources
    tops = jnp.where(there, gathered(0, 3), -jnp.inf)
    weights = jnp.exp(tops - jnp.max(tops, -1, keepdims=True))
    total = jnp.sum(weights * gathered(3, 5), -1, keepdims=True)
    accum = jnp.zeros((count, HEAD_SIZE), jnp.float32)
    for at in range(sources):
        accum += weights[:, at : at + 1] * got_ref[at, :count, :].astype(jnp.float32)
    attended = accum / total
    head = lax.broadcasted_iota(jnp.int32, (count, HEAD_SIZE), 0) % QUERY_GROUP
    spread = jnp.concatenate(
        [jnp.where(head == at, attended, 0.0).astype(jnp.bfloat16) for at in range(QUERY_GROUP)], 1
    )
    product = jnp.dot(spread, output_ref[...], preferred_element_type=jnp.float32)
    out_ref[...] = jnp.sum(product.reshape(batch, QUERY_GROUP, HEAD_SIZE), 1)


def frequencies():
    exponent = jnp.arange(0, HEAD_SIZE, 2).astype(jnp.float32) / HEAD_SIZE
    return jnp.power(rope_theta, -exponent)


def local(
    token_input_state,
    query_matrix,
    key_value_weight,
    output_weight,
    key_cache_rows,
    value_cache_rows,
    live_lengths,
    owner_shard,
):
    batch_rows = token_input_state.shape[0]
    row_count = query_matrix.shape[0]
    shard_index = lax.axis_index(SEQ)
    heads = QUERY_GROUP + 2
    rows = batch_rows * heads
    exponent = jnp.arange(0, HEAD_SIZE, 2).astype(jnp.float32) / HEAD_SIZE
    rates = jnp.power(rope_theta, -exponent)
    rates = jnp.concatenate([rates, rates]).reshape(1, HEAD_SIZE)
    index, rates = lax.optimization_barrier((shard_index.reshape(1), rates))
    copies = pl.pallas_call(
        project_kernel,
        out_shape=pltpu.VMEM((lax.axis_size(SEQ[1:]), rows, HEAD_SIZE), jnp.float32),
        in_specs=[smem(), hbm(), hbm(), hbm()],
        out_specs=vmem(),
        scratch_shapes=[
            pltpu.VMEM((batch_rows, row_count), jnp.bfloat16),
            pltpu.VMEM(query_matrix.shape, jnp.bfloat16),
            pltpu.VMEM(key_value_weight.shape, jnp.bfloat16),
            pltpu.SemaphoreType.DMA((3,)),
        ],
        compiler_params=pltpu.CompilerParams(vmem_limit_bytes=8 << 20),
        name="project",
    )(index, left(token_input_state), left(query_matrix), left(key_value_weight))
    planes = range(0, lax.axis_size(SEQ), len(MIXED_PLANE))
    groups = [[plane + chip for chip in MIXED_PLANE] for plane in planes]
    got = lax.all_to_all(copies, SEQ, 0, 0, tiled=True, axis_index_groups=groups)
    got, later_index, rates = lax.optimization_barrier((got, index, rates))
    parts = got.sum(0)
    beside, around, across = exchanges(parts, SEQ[0])
    caches = (key_cache_rows, value_cache_rows, output_weight)
    table = pltpu.VMEM((2 * batch_rows, HEAD_SIZE), jnp.float32)
    places = pltpu.VMEM((2 * batch_rows, HEAD_SIZE), jnp.int32)
    keys, values, outputs, cosine, sine, own = pl.pallas_call(
        prepare_kernel,
        out_shape=[*(pltpu.VMEM(a.shape, a.dtype) for a in caches), table, table, places],
        in_specs=[smem()] * 3 + [vmem()] + [hbm()] * 3,
        out_specs=[vmem()] * 6,
        scratch_shapes=[pltpu.SemaphoreType.DMA((2 * batch_rows + 1,))],
        compiler_params=pltpu.CompilerParams(vmem_limit_bytes=8 << 20),
        name="prepare",
    )(
        later_index,
        left(live_lengths),
        left(owner_shard),
        rates,
        *(left(a) for a in caches),
    )
    count = batch_rows * QUERY_GROUP
    message = pl.pallas_call(
        attend_kernel,
        out_shape=pltpu.VMEM((lax.axis_size(SEQ), count + QUERY_GROUP, HEAD_SIZE), jnp.bfloat16),
        in_specs=[vmem()] * 9,
        out_specs=vmem(),
        scratch_shapes=[pltpu.VMEM((rows, HEAD_SIZE), jnp.float32)],
        compiler_params=pltpu.CompilerParams(vmem_limit_bytes=8 << 20),
        name="attend",
    )(
        *(held(a) for a in (parts, beside, around, across, cosine, sine, own, keys, values)),
    )
    got = lax.all_to_all(message, SEQ, 0, 0, tiled=True, axis_index_groups=[list(MIXED)])
    partial_value = pl.pallas_call(
        merge_kernel,
        out_shape=pltpu.VMEM((batch_rows, HEAD_SIZE), jnp.float32),
        in_specs=[vmem()] * 2,
        out_specs=vmem(),
        compiler_params=pltpu.CompilerParams(vmem_limit_bytes=8 << 20),
        name="merge",
    )(held(got), held(outputs))
    other = lax.ppermute(partial_value, "kv", ((0, 1), (1, 0)))
    return (partial_value + other).astype(jnp.bfloat16)


def solution(mesh):
    finer = Mesh(
        mesh.devices.reshape(mesh.shape["kv"], 4, 4, 4, mesh.shape["dp"]),
        ("kv", "seq_0", "seq_1", "seq_2", "dp"),
    )
    return jax.shard_map(
        local,
        mesh=finer,
        in_specs=(
            P("dp", None),
            P(SEQ, "kv"),
            P(SEQ, "kv"),
            P("kv", SEQ),
            P("dp", "kv", SEQ, None),
            P("dp", "kv", SEQ, None),
            P("dp", None),
            P("dp"),
        ),
        out_specs=P("dp", SEQ),
        check_vma=False,
    )
```

```python
import math

import jax
import jax.numpy as jnp
from jax import lax
from jax.experimental import pallas as pl
from jax.experimental.pallas import tpu as pltpu
from jax.sharding import Mesh
from jax.sharding import PartitionSpec as P

HEAD_SIZE = 128
QUERY_GROUP = 8
SEQ = ("seq_0", "seq_1", "seq_2")
MIXED_PLANE = (10, 8, 12, 1, 2, 5, 9, 15, 0, 13, 3, 6, 4, 14, 7, 11)
MIXED = [(at + turn) % 4 * 16 + chip for at, chip in enumerate(MIXED_PLANE) for turn in range(4)]


rope_theta = 500000.0


def exchanges(array, axis):
    beside = lax.ppermute(array, axis, ((0, 1), (1, 2), (2, 3), (3, 0)))
    around = lax.ppermute(array, axis, ((0, 3), (1, 0), (2, 1), (3, 2)))
    across = lax.ppermute(array, axis, ((0, 2), (2, 0), (1, 3), (3, 1)))
    return beside, around, across


def held(array):
    return pltpu.with_memory_space_constraint(array, pltpu.VMEM)


def left(array):
    return pltpu.with_memory_space_constraint(array, pltpu.HBM)


def vmem():
    return pl.BlockSpec(memory_space=pltpu.VMEM)


def hbm():
    return pl.BlockSpec(memory_space=pltpu.HBM)


def smem():
    return pl.BlockSpec(memory_space=pltpu.SMEM)


def project_kernel(shard_ref, state_ref, query_ref, keyval_ref, out_ref, state_v, query_v, keyval_v, sems):
    columns = pl.ds(pl.multiple_of(shard_ref[0] * query_v.shape[0], query_v.shape[0]), query_v.shape[0])
    loads = [
        pltpu.make_async_copy(query_ref, query_v, sems.at[0]),
        pltpu.make_async_copy(keyval_ref, keyval_v, sems.at[1]),
        pltpu.make_async_copy(state_ref.at[:, columns], state_v, sems.at[2]),
    ]
    for load in loads:
        load.start()
    for load in loads:
        load.wait()
    state = state_v[...]
    parts = []
    for weights in (query_v, keyval_v):
        product = jnp.dot(state, weights[...], preferred_element_type=jnp.float32)
        parts += [product[:, at : at + HEAD_SIZE] for at in range(0, product.shape[1], HEAD_SIZE)]
    rows = jnp.concatenate(parts, 0)
    for copy in range(out_ref.shape[0]):
        out_ref[copy] = rows


def prepare_kernel(
    shard_ref, live_ref, owner_ref, rate_ref, key_ref, value_ref, output_ref,
    key_out, value_out, output_out, cosine_ref, sine_ref, own_ref, sems,
):
    batch, _, slots, _ = key_ref.shape
    loads = [pltpu.make_async_copy(output_ref, output_out, sems.at[2 * batch])]
    for b in range(batch):
        loads.append(pltpu.make_async_copy(key_ref.at[b], key_out.at[b], sems.at[b]))
        loads.append(pltpu.make_async_copy(value_ref.at[b], value_out.at[b], sems.at[batch + b]))
    for load in loads:
        load.start()
    sublane = lax.broadcasted_iota(jnp.int32, (2 * batch, HEAD_SIZE), 0)
    lane = lax.broadcasted_iota(jnp.int32, (2 * batch, HEAD_SIZE), 1)
    place = jnp.zeros((2 * batch, HEAD_SIZE), jnp.int32)
    own = place
    for b in range(batch):
        position = owner_ref[b] * slots + live_ref[b, owner_ref[b]]
        place = jnp.where(sublane % batch == b, position, place)
        own = jnp.where(sublane == b, live_ref[b, shard_ref[0]], own)
        own = jnp.where(sublane == b + batch, jnp.where(owner_ref[b] == shard_ref[0], 1, 0), own)
    own_ref[...] = own
    angle = place.astype(jnp.float32) * rate_ref[...]
    cosine_ref[...] = jnp.cos(angle)
    sine = jnp.sin(angle)
    sine_ref[...] = jnp.where(lane < HEAD_SIZE // 2, -sine, sine)
    for load in loads:
        load.wait()


def attend_kernel(
    part_ref, beside_ref, around_ref, across_ref, cosine_ref, sine_ref, own_ref,
    key_ref, value_ref, out_ref, score_ref,
):
    batch, _, slots, _ = key_ref.shape
    cosine, sine = cosine_ref[...], sine_ref[...]
    straight = lax.broadcasted_iota(jnp.int32, cosine.shape, 0) >= batch
    for at in range(0, score_ref.shape[0], 2 * batch):
        tile = pl.ds(at, 2 * batch)
        total = (part_ref[tile, :] + across_ref[tile, :]) + (beside_ref[tile, :] + around_ref[tile, :])
        if at + 2 * batch == score_ref.shape[0]:
            cosine = jnp.where(straight, 1.0, cosine)
            sine = jnp.where(straight, 0.0, sine)
        turned = total * cosine + pltpu.roll(total, HEAD_SIZE // 2, 1) * sine
        score_ref[tile, :] = turned
    scaling = 1.0 / math.sqrt(HEAD_SIZE)
    lane = lax.broadcasted_iota(jnp.int32, (QUERY_GROUP, HEAD_SIZE), 1)
    sublane = lax.broadcasted_iota(jnp.int32, (QUERY_GROUP, HEAD_SIZE), 0)
    top_row = jnp.zeros((1, HEAD_SIZE), jnp.float32)
    total_row = jnp.zeros((1, HEAD_SIZE), jnp.float32)
    picks = []
    for b in range(batch):
        query = score_ref[pl.ds(b, QUERY_GROUP, stride=batch), :].astype(jnp.bfloat16)
        key_new = turned[b : b + 1].astype(jnp.bfloat16)
        value_new = turned[batch + b : batch + b + 1].astype(jnp.bfloat16)
        picks.append((query, key_new.astype(jnp.float32), value_new.astype(jnp.float32)))
    slot = lax.broadcasted_iota(jnp.int32, (QUERY_GROUP, slots), 1)
    scores_of = [
        lax.dot_general(query, key_ref[b, 0], (((1,), (1,)), ((), ())), preferred_element_type=jnp.float32)
        * scaling
        for b, (query, _, _) in enumerate(picks)
    ]
    probs, additions = [], []
    for b, (query, key_new, value_new) in enumerate(picks):
        scores = jnp.where(slot < own_ref[b : b + 1, 0:1], scores_of[b], -jnp.inf)
        new_score = jnp.sum(query.astype(jnp.float32) * key_new, -1, keepdims=True) * scaling
        owns = own_ref[batch + b : batch + b + 1, 0:1] > 0
        top = jnp.maximum(jnp.max(scores, -1, keepdims=True), jnp.where(owns, new_score, -jnp.inf))
        prob = jnp.exp(scores - top).astype(jnp.bfloat16)
        new_prob = jnp.where(owns, jnp.exp(new_score - top), 0.0).astype(jnp.bfloat16).astype(jnp.float32)
        weight = jnp.sum(prob.astype(jnp.float32), -1, keepdims=True) + new_prob
        probs.append(prob)
        additions.append(new_prob * value_new)
        mine = lane == sublane + b * QUERY_GROUP
        top_row += jnp.sum(jnp.where(mine, top, 0.0), 0, keepdims=True)
        total_row += jnp.sum(jnp.where(mine, weight, 0.0), 0, keepdims=True)
    accums = [
        jnp.dot(prob, value_ref[b, 0], preferred_element_type=jnp.float32) + additions[b]
        for b, prob in enumerate(probs)
    ]
    side = jnp.zeros((QUERY_GROUP, HEAD_SIZE), jnp.float32)
    at = 0
    for row, count in ((top_row, 3), (total_row, 2)):
        for _ in range(count):
            piece = row.astype(jnp.bfloat16).astype(jnp.float32)
            side = jnp.where(sublane == at, piece, side)
            row = row - piece
            at += 1
    message = jnp.concatenate(accums + [side], 0).astype(jnp.bfloat16)
    for copy in range(out_ref.shape[0]):
        out_ref[copy] = message


def merge_kernel(got_ref, output_ref, out_ref):
    sources = got_ref.shape[0]
    batch = out_ref.shape[0]
    count = batch * QUERY_GROUP
    side = got_ref[:, count:, :].astype(jnp.float32).reshape(sources * QUERY_GROUP, HEAD_SIZE).astype(jnp.bfloat16)
    source = lax.broadcasted_iota(jnp.int32, (2 * sources, sources * QUERY_GROUP), 0)
    entry = lax.broadcasted_iota(jnp.int32, (2 * sources, sources * QUERY_GROUP), 1)
    place = entry - source * QUERY_GROUP
    of_total = place + sources * QUERY_GROUP
    chosen = ((place >= 0) & (place < 3)) | ((of_total >= 3) & (of_total < 5))
    chosen = chosen.astype(jnp.float32).astype(jnp.bfloat16)
    found = jnp.dot(chosen, side, preferred_element_type=jnp.float32).T[:count]
    tops, totals = found[:, :sources], found[:, sources:]
    weights = jnp.exp(tops - jnp.max(tops, -1, keepdims=True))
    total = jnp.sum(weights * totals, -1, keepdims=True)
    accum = jnp.zeros((count, HEAD_SIZE), jnp.float32)
    for at in range(sources):
        accum += weights[:, at : at + 1] * got_ref[at, :count, :].astype(jnp.float32)
    attended = accum / total
    head = lax.broadcasted_iota(jnp.int32, (count, HEAD_SIZE), 0) % QUERY_GROUP
    spread = jnp.concatenate(
        [jnp.where(head == at, attended, 0.0).astype(jnp.bfloat16) for at in range(QUERY_GROUP)], 1
    )
    product = jnp.dot(spread, output_ref[...], preferred_element_type=jnp.float32)
    out_ref[...] = jnp.sum(product.reshape(batch, QUERY_GROUP, HEAD_SIZE), 1)


def merge_kernel(got_ref, output_ref, out_ref):
    sources = got_ref.shape[0]
    batch = out_ref.shape[0]
    count = batch * QUERY_GROUP
    side = got_ref[:, count:, :].astype(jnp.float32).reshape(sources * QUERY_GROUP, HEAD_SIZE).astype(jnp.bfloat16)
    source = lax.broadcasted_iota(jnp.int32, (HEAD_SIZE, sources * QUERY_GROUP), 0)
    entry = lax.broadcasted_iota(jnp.int32, (HEAD_SIZE, sources * QUERY_GROUP), 1)
    place = entry - source * QUERY_GROUP

    def gathered(low, high):
        chosen = ((place >= low) & (place < high)).astype(jnp.float32).astype(jnp.bfloat16)
        return jnp.dot(chosen, side, preferred_element_type=jnp.float32).T[:count]

    there = lax.broadcasted_iota(jnp.int32, (count, HEAD_SIZE), 1) < sources
    tops = jnp.where(there, gathered(0, 3), -jnp.inf)
    weights = jnp.exp(tops - jnp.max(tops, -1, keepdims=True))
    total = jnp.sum(weights * gathered(3, 5), -1, keepdims=True)
    accum = jnp.zeros((count, HEAD_SIZE), jnp.float32)
    for at in range(sources):
        accum += weights[:, at : at + 1] * got_ref[at, :count, :].astype(jnp.float32)
    attended = accum / total
    head = lax.broadcasted_iota(jnp.int32, (count, HEAD_SIZE), 0) % QUERY_GROUP
    spread = jnp.concatenate(
        [jnp.where(head == at, attended, 0.0).astype(jnp.bfloat16) for at in range(QUERY_GROUP)], 1
    )
    product = jnp.dot(spread, output_ref[...], preferred_element_type=jnp.float32)
    out_ref[...] = jnp.sum(product.reshape(batch, QUERY_GROUP, HEAD_SIZE), 1)


def frequencies():
    exponent = jnp.arange(0, HEAD_SIZE, 2).astype(jnp.float32) / HEAD_SIZE
    return jnp.power(rope_theta, -exponent)


def local(
    token_input_state,
    query_matrix,
    key_value_weight,
    output_weight,
    key_cache_rows,
    value_cache_rows,
    live_lengths,
    owner_shard,
):
    batch_rows = token_input_state.shape[0]
    row_count = query_matrix.shape[0]
    shard_index = lax.axis_index(SEQ)
    heads = QUERY_GROUP + 2
    rows = batch_rows * heads
    exponent = jnp.arange(0, HEAD_SIZE, 2).astype(jnp.float32) / HEAD_SIZE
    rates = jnp.power(rope_theta, -exponent)
    rates = jnp.concatenate([rates, rates]).reshape(1, HEAD_SIZE)
    index, rates = lax.optimization_barrier((shard_index.reshape(1), rates))
    copies = pl.pallas_call(
        project_kernel,
        out_shape=pltpu.VMEM((lax.axis_size(SEQ[1:]), rows, HEAD_SIZE), jnp.float32),
        in_specs=[smem(), hbm(), hbm(), hbm()],
        out_specs=vmem(),
        scratch_shapes=[
            pltpu.VMEM((batch_rows, row_count), jnp.bfloat16),
            pltpu.VMEM(query_matrix.shape, jnp.bfloat16),
            pltpu.VMEM(key_value_weight.shape, jnp.bfloat16),
            pltpu.SemaphoreType.DMA((3,)),
        ],
        compiler_params=pltpu.CompilerParams(vmem_limit_bytes=8 << 20),
        name="project",
    )(index, left(token_input_state), left(query_matrix), left(key_value_weight))
    planes = range(0, lax.axis_size(SEQ), len(MIXED_PLANE))
    groups = [[plane + chip for chip in MIXED_PLANE] for plane in planes]
    got = lax.all_to_all(copies, SEQ, 0, 0, tiled=True, axis_index_groups=groups)
    got, later_index, rates = lax.optimization_barrier((got, index, rates))
    parts = got.sum(0)
    beside, around, across = exchanges(parts, SEQ[0])
    caches = (key_cache_rows, value_cache_rows, output_weight)
    table = pltpu.VMEM((2 * batch_rows, HEAD_SIZE), jnp.float32)
    places = pltpu.VMEM((2 * batch_rows, HEAD_SIZE), jnp.int32)
    keys, values, outputs, cosine, sine, own = pl.pallas_call(
        prepare_kernel,
        out_shape=[*(pltpu.VMEM(a.shape, a.dtype) for a in caches), table, table, places],
        in_specs=[smem()] * 3 + [vmem()] + [hbm()] * 3,
        out_specs=[vmem()] * 6,
        scratch_shapes=[pltpu.SemaphoreType.DMA((2 * batch_rows + 1,))],
        compiler_params=pltpu.CompilerParams(vmem_limit_bytes=8 << 20),
        name="prepare",
    )(
        later_index,
        left(live_lengths),
        left(owner_shard),
        rates,
        *(left(a) for a in caches),
    )
    count = batch_rows * QUERY_GROUP
    message = pl.pallas_call(
        attend_kernel,
        out_shape=pltpu.VMEM((lax.axis_size(SEQ), count + QUERY_GROUP, HEAD_SIZE), jnp.bfloat16),
        in_specs=[vmem()] * 9,
        out_specs=vmem(),
        scratch_shapes=[pltpu.VMEM((rows, HEAD_SIZE), jnp.float32)],
        compiler_params=pltpu.CompilerParams(vmem_limit_bytes=8 << 20),
        name="attend",
    )(
        *(held(a) for a in (parts, beside, around, across, cosine, sine, own, keys, values)),
    )
    got = lax.all_to_all(message, SEQ, 0, 0, tiled=True, axis_index_groups=[MIXED])
    partial_value = pl.pallas_call(
        merge_kernel,
        out_shape=pltpu.VMEM((batch_rows, HEAD_SIZE), jnp.float32),
        in_specs=[vmem()] * 2,
        out_specs=vmem(),
        compiler_params=pltpu.CompilerParams(vmem_limit_bytes=8 << 20),
        name="merge",
    )(held(got), held(outputs))
    other = lax.ppermute(partial_value, "kv", ((0, 1), (1, 0)))
    return (partial_value + other).astype(jnp.bfloat16)


def solution(mesh):
    finer = Mesh(
        mesh.devices.reshape(mesh.shape["kv"], 4, 4, 4, mesh.shape["dp"]),
        ("kv", "seq_0", "seq_1", "seq_2", "dp"),
    )
    return jax.shard_map(
        local,
        mesh=finer,
        in_specs=(
            P("dp", None),
            P(SEQ, "kv"),
            P(SEQ, "kv"),
            P("kv", SEQ),
            P("dp", "kv", SEQ, None),
            P("dp", "kv", SEQ, None),
            P("dp", None),
            P("dp"),
        ),
        out_specs=P("dp", SEQ),
        check_vma=False,
    )
```

```python
import math

import jax
import jax.numpy as jnp
from jax import lax
from jax.experimental import pallas as pl
from jax.experimental.pallas import tpu as pltpu
from jax.sharding import Mesh
from jax.sharding import PartitionSpec as P

HEAD_SIZE = 128
QUERY_GROUP = 8
SEQ = ("seq_0", "seq_1", "seq_2")
MIXED_PLANE = (10, 8, 12, 1, 2, 5, 9, 15, 0, 13, 3, 6, 4, 14, 7, 11)
FIRST_PLANE = (10, 14, 5, 1, 9, 2, 3, 11, 13, 7, 8, 4, 0, 6, 15, 12)
MIXED = [(at + turn) % 4 * 16 + chip for at, chip in enumerate(MIXED_PLANE) for turn in range(4)]


rope_theta = 500000.0


def exchanges(array, axis):
    beside = lax.ppermute(array, axis, ((0, 1), (1, 2), (2, 3), (3, 0)))
    around = lax.ppermute(array, axis, ((0, 3), (1, 0), (2, 1), (3, 2)))
    across = lax.ppermute(array, axis, ((0, 2), (2, 0), (1, 3), (3, 1)))
    return beside, around, across


def held(array):
    return pltpu.with_memory_space_constraint(array, pltpu.VMEM)


def left(array):
    return pltpu.with_memory_space_constraint(array, pltpu.HBM)


def vmem():
    return pl.BlockSpec(memory_space=pltpu.VMEM)


def hbm():
    return pl.BlockSpec(memory_space=pltpu.HBM)


def smem():
    return pl.BlockSpec(memory_space=pltpu.SMEM)


def project_kernel(shard_ref, state_ref, query_ref, keyval_ref, out_ref, state_v, query_v, keyval_v, sems):
    columns = pl.ds(pl.multiple_of(shard_ref[0] * query_v.shape[0], query_v.shape[0]), query_v.shape[0])
    loads = [
        pltpu.make_async_copy(query_ref, query_v, sems.at[0]),
        pltpu.make_async_copy(keyval_ref, keyval_v, sems.at[1]),
        pltpu.make_async_copy(state_ref.at[:, columns], state_v, sems.at[2]),
    ]
    for load in loads:
        load.start()
    for load in loads:
        load.wait()
    state = state_v[...]
    parts = []
    for weights in (query_v, keyval_v):
        product = jnp.dot(state, weights[...], preferred_element_type=jnp.float32)
        parts += [product[:, at : at + HEAD_SIZE] for at in range(0, product.shape[1], HEAD_SIZE)]
    rows = jnp.concatenate(parts, 0)
    for copy in range(out_ref.shape[0]):
        out_ref[copy] = rows


def prepare_kernel(
    shard_ref, live_ref, owner_ref, rate_ref, key_ref, value_ref, output_ref,
    key_out, value_out, output_out, cosine_ref, sine_ref, own_ref, sems,
):
    batch, _, slots, _ = key_ref.shape
    loads = [pltpu.make_async_copy(output_ref, output_out, sems.at[2 * batch])]
    for b in range(batch):
        loads.append(pltpu.make_async_copy(key_ref.at[b], key_out.at[b], sems.at[b]))
        loads.append(pltpu.make_async_copy(value_ref.at[b], value_out.at[b], sems.at[batch + b]))
    for load in loads:
        load.start()
    sublane = lax.broadcasted_iota(jnp.int32, (2 * batch, HEAD_SIZE), 0)
    lane = lax.broadcasted_iota(jnp.int32, (2 * batch, HEAD_SIZE), 1)
    place = jnp.zeros((2 * batch, HEAD_SIZE), jnp.int32)
    own = place
    for b in range(batch):
        position = owner_ref[b] * slots + live_ref[b, owner_ref[b]]
        place = jnp.where(sublane % batch == b, position, place)
        own = jnp.where(sublane == b, live_ref[b, shard_ref[0]], own)
        own = jnp.where(sublane == b + batch, jnp.where(owner_ref[b] == shard_ref[0], 1, 0), own)
    own_ref[...] = own
    angle = place.astype(jnp.float32) * rate_ref[...]
    cosine_ref[...] = jnp.cos(angle)
    sine = jnp.sin(angle)
    sine_ref[...] = jnp.where(lane < HEAD_SIZE // 2, -sine, sine)
    for load in loads:
        load.wait()


def attend_kernel(
    part_ref, beside_ref, around_ref, across_ref, cosine_ref, sine_ref, own_ref,
    key_ref, value_ref, out_ref, score_ref,
):
    batch, _, slots, _ = key_ref.shape
    cosine, sine = cosine_ref[...], sine_ref[...]
    straight = lax.broadcasted_iota(jnp.int32, cosine.shape, 0) >= batch
    for at in range(0, score_ref.shape[0], 2 * batch):
        tile = pl.ds(at, 2 * batch)
        total = (part_ref[tile, :] + across_ref[tile, :]) + (beside_ref[tile, :] + around_ref[tile, :])
        if at + 2 * batch == score_ref.shape[0]:
            cosine = jnp.where(straight, 1.0, cosine)
            sine = jnp.where(straight, 0.0, sine)
        turned = total * cosine + pltpu.roll(total, HEAD_SIZE // 2, 1) * sine
        score_ref[tile, :] = turned
    scaling = 1.0 / math.sqrt(HEAD_SIZE)
    lane = lax.broadcasted_iota(jnp.int32, (QUERY_GROUP, HEAD_SIZE), 1)
    sublane = lax.broadcasted_iota(jnp.int32, (QUERY_GROUP, HEAD_SIZE), 0)
    top_row = jnp.zeros((1, HEAD_SIZE), jnp.float32)
    total_row = jnp.zeros((1, HEAD_SIZE), jnp.float32)
    picks = []
    for b in range(batch):
        query = score_ref[pl.ds(b, QUERY_GROUP, stride=batch), :].astype(jnp.bfloat16)
        key_new = turned[b : b + 1].astype(jnp.bfloat16)
        value_new = turned[batch + b : batch + b + 1].astype(jnp.bfloat16)
        picks.append((query, key_new.astype(jnp.float32), value_new.astype(jnp.float32)))
    slot = lax.broadcasted_iota(jnp.int32, (QUERY_GROUP, slots), 1)
    scores_of = [
        lax.dot_general(query, key_ref[b, 0], (((1,), (1,)), ((), ())), preferred_element_type=jnp.float32)
        * scaling
        for b, (query, _, _) in enumerate(picks)
    ]
    probs, additions = [], []
    for b, (query, key_new, value_new) in enumerate(picks):
        scores = jnp.where(slot < own_ref[b : b + 1, 0:1], scores_of[b], -jnp.inf)
        new_score = jnp.sum(query.astype(jnp.float32) * key_new, -1, keepdims=True) * scaling
        owns = own_ref[batch + b : batch + b + 1, 0:1] > 0
        top = jnp.maximum(jnp.max(scores, -1, keepdims=True), jnp.where(owns, new_score, -jnp.inf))
        prob = jnp.exp(scores - top).astype(jnp.bfloat16)
        new_prob = jnp.where(owns, jnp.exp(new_score - top), 0.0).astype(jnp.bfloat16).astype(jnp.float32)
        weight = jnp.sum(prob.astype(jnp.float32), -1, keepdims=True) + new_prob
        probs.append(prob)
        additions.append(new_prob * value_new)
        mine = lane == sublane + b * QUERY_GROUP
        top_row += jnp.sum(jnp.where(mine, top, 0.0), 0, keepdims=True)
        total_row += jnp.sum(jnp.where(mine, weight, 0.0), 0, keepdims=True)
    accums = [
        jnp.dot(prob, value_ref[b, 0], preferred_element_type=jnp.float32) + additions[b]
        for b, prob in enumerate(probs)
    ]
    side = jnp.zeros((QUERY_GROUP, HEAD_SIZE), jnp.float32)
    at = 0
    for row, count in ((top_row, 3), (total_row, 2)):
        for _ in range(count):
            piece = row.astype(jnp.bfloat16).astype(jnp.float32)
            side = jnp.where(sublane == at, piece, side)
            row = row - piece
            at += 1
    message = jnp.concatenate(accums + [side], 0).astype(jnp.bfloat16)
    for copy in range(out_ref.shape[0]):
        out_ref[copy] = message


def merge_kernel(got_ref, output_ref, out_ref):
    sources = got_ref.shape[0]
    batch = out_ref.shape[0]
    count = batch * QUERY_GROUP
    side = got_ref[:, count:, :].astype(jnp.float32).reshape(sources * QUERY_GROUP, HEAD_SIZE).astype(jnp.bfloat16)
    source = lax.broadcasted_iota(jnp.int32, (2 * sources, sources * QUERY_GROUP), 0)
    entry = lax.broadcasted_iota(jnp.int32, (2 * sources, sources * QUERY_GROUP), 1)
    place = entry - source * QUERY_GROUP
    of_total = place + sources * QUERY_GROUP
    chosen = ((place >= 0) & (place < 3)) | ((of_total >= 3) & (of_total < 5))
    chosen = chosen.astype(jnp.float32).astype(jnp.bfloat16)
    found = jnp.dot(chosen, side, preferred_element_type=jnp.float32).T[:count]
    tops, totals = found[:, :sources], found[:, sources:]
    weights = jnp.exp(tops - jnp.max(tops, -1, keepdims=True))
    total = jnp.sum(weights * totals, -1, keepdims=True)
    accum = jnp.zeros((count, HEAD_SIZE), jnp.float32)
    for at in range(sources):
        accum += weights[:, at : at + 1] * got_ref[at, :count, :].astype(jnp.float32)
    attended = accum / total
    head = lax.broadcasted_iota(jnp.int32, (count, HEAD_SIZE), 0) % QUERY_GROUP
    spread = jnp.concatenate(
        [jnp.where(head == at, attended, 0.0).astype(jnp.bfloat16) for at in range(QUERY_GROUP)], 1
    )
    product = jnp.dot(spread, output_ref[...], preferred_element_type=jnp.float32)
    out_ref[...] = jnp.sum(product.reshape(batch, QUERY_GROUP, HEAD_SIZE), 1)


def merge_kernel(got_ref, output_ref, out_ref):
    sources = got_ref.shape[0]
    batch = out_ref.shape[0]
    count = batch * QUERY_GROUP
    side = got_ref[:, count:, :].astype(jnp.float32).reshape(sources * QUERY_GROUP, HEAD_SIZE).astype(jnp.bfloat16)
    source = lax.broadcasted_iota(jnp.int32, (HEAD_SIZE, sources * QUERY_GROUP), 0)
    entry = lax.broadcasted_iota(jnp.int32, (HEAD_SIZE, sources * QUERY_GROUP), 1)
    place = entry - source * QUERY_GROUP

    def gathered(low, high):
        chosen = ((place >= low) & (place < high)).astype(jnp.float32).astype(jnp.bfloat16)
        return jnp.dot(chosen, side, preferred_element_type=jnp.float32).T[:count]

    there = lax.broadcasted_iota(jnp.int32, (count, HEAD_SIZE), 1) < sources
    tops = jnp.where(there, gathered(0, 3), -jnp.inf)
    weights = jnp.exp(tops - jnp.max(tops, -1, keepdims=True))
    total = jnp.sum(weights * gathered(3, 5), -1, keepdims=True)
    accum = jnp.zeros((count, HEAD_SIZE), jnp.float32)
    for at in range(sources):
        accum += weights[:, at : at + 1] * got_ref[at, :count, :].astype(jnp.float32)
    attended = accum / total
    head = lax.broadcasted_iota(jnp.int32, (count, HEAD_SIZE), 0) % QUERY_GROUP
    spread = jnp.concatenate(
        [jnp.where(head == at, attended, 0.0).astype(jnp.bfloat16) for at in range(QUERY_GROUP)], 1
    )
    product = jnp.dot(spread, output_ref[...], preferred_element_type=jnp.float32)
    out_ref[...] = jnp.sum(product.reshape(batch, QUERY_GROUP, HEAD_SIZE), 1)


def frequencies():
    exponent = jnp.arange(0, HEAD_SIZE, 2).astype(jnp.float32) / HEAD_SIZE
    return jnp.power(rope_theta, -exponent)


def local(
    token_input_state,
    query_matrix,
    key_value_weight,
    output_weight,
    key_cache_rows,
    value_cache_rows,
    live_lengths,
    owner_shard,
):
    batch_rows = token_input_state.shape[0]
    row_count = query_matrix.shape[0]
    shard_index = lax.axis_index(SEQ)
    heads = QUERY_GROUP + 2
    rows = batch_rows * heads
    exponent = jnp.arange(0, HEAD_SIZE, 2).astype(jnp.float32) / HEAD_SIZE
    rates = jnp.power(rope_theta, -exponent)
    rates = jnp.concatenate([rates, rates]).reshape(1, HEAD_SIZE)
    index, rates = lax.optimization_barrier((shard_index.reshape(1), rates))
    copies = pl.pallas_call(
        project_kernel,
        out_shape=pltpu.VMEM((lax.axis_size(SEQ[1:]), rows, HEAD_SIZE), jnp.float32),
        in_specs=[smem(), hbm(), hbm(), hbm()],
        out_specs=vmem(),
        scratch_shapes=[
            pltpu.VMEM((batch_rows, row_count), jnp.bfloat16),
            pltpu.VMEM(query_matrix.shape, jnp.bfloat16),
            pltpu.VMEM(key_value_weight.shape, jnp.bfloat16),
            pltpu.SemaphoreType.DMA((3,)),
        ],
        compiler_params=pltpu.CompilerParams(vmem_limit_bytes=8 << 20),
        name="project",
    )(index, left(token_input_state), left(query_matrix), left(key_value_weight))
    planes = range(0, lax.axis_size(SEQ), len(FIRST_PLANE))
    groups = [[plane + chip for chip in FIRST_PLANE] for plane in planes]
    got = lax.all_to_all(copies, SEQ, 0, 0, tiled=True, axis_index_groups=groups)
    got, later_index, rates = lax.optimization_barrier((got, index, rates))
    parts = got.sum(0)
    beside, around, across = exchanges(parts, SEQ[0])
    caches = (key_cache_rows, value_cache_rows, output_weight)
    table = pltpu.VMEM((2 * batch_rows, HEAD_SIZE), jnp.float32)
    places = pltpu.VMEM((2 * batch_rows, HEAD_SIZE), jnp.int32)
    keys, values, outputs, cosine, sine, own = pl.pallas_call(
        prepare_kernel,
        out_shape=[*(pltpu.VMEM(a.shape, a.dtype) for a in caches), table, table, places],
        in_specs=[smem()] * 3 + [vmem()] + [hbm()] * 3,
        out_specs=[vmem()] * 6,
        scratch_shapes=[pltpu.SemaphoreType.DMA((2 * batch_rows + 1,))],
        compiler_params=pltpu.CompilerParams(vmem_limit_bytes=8 << 20),
        name="prepare",
    )(
        later_index,
        left(live_lengths),
        left(owner_shard),
        rates,
        *(left(a) for a in caches),
    )
    count = batch_rows * QUERY_GROUP
    message = pl.pallas_call(
        attend_kernel,
        out_shape=pltpu.VMEM((lax.axis_size(SEQ), count + QUERY_GROUP, HEAD_SIZE), jnp.bfloat16),
        in_specs=[vmem()] * 9,
        out_specs=vmem(),
        scratch_shapes=[pltpu.VMEM((rows, HEAD_SIZE), jnp.float32)],
        compiler_params=pltpu.CompilerParams(vmem_limit_bytes=8 << 20),
        name="attend",
    )(
        *(held(a) for a in (parts, beside, around, across, cosine, sine, own, keys, values)),
    )
    got = lax.all_to_all(message, SEQ, 0, 0, tiled=True, axis_index_groups=[MIXED])
    partial_value = pl.pallas_call(
        merge_kernel,
        out_shape=pltpu.VMEM((batch_rows, HEAD_SIZE), jnp.float32),
        in_specs=[vmem()] * 2,
        out_specs=vmem(),
        compiler_params=pltpu.CompilerParams(vmem_limit_bytes=8 << 20),
        name="merge",
    )(held(got), held(outputs))
    other = lax.ppermute(partial_value, "kv", ((0, 1), (1, 0)))
    return (partial_value + other).astype(jnp.bfloat16)


def solution(mesh):
    finer = Mesh(
        mesh.devices.reshape(mesh.shape["kv"], 4, 4, 4, mesh.shape["dp"]),
        ("kv", "seq_0", "seq_1", "seq_2", "dp"),
    )
    return jax.shard_map(
        local,
        mesh=finer,
        in_specs=(
            P("dp", None),
            P(SEQ, "kv"),
            P(SEQ, "kv"),
            P("kv", SEQ),
            P("dp", "kv", SEQ, None),
            P("dp", "kv", SEQ, None),
            P("dp", None),
            P("dp"),
        ),
        out_specs=P("dp", SEQ),
        check_vma=False,
    )
```
